32 devices in a mesh: layer: 4 (over y, x), strip: 8 (over z, core).
Axes of the slice: x: 2, y: 2, z: 4, core: 2. Of those that a mesh axis runs over, the one named last changes fastest.
Arguments:
- launch: bfloat16 [2, 2, 1024, 1024], P(None, None, 'strip'), may hold values from -6 to 6
- screens: float32 [4, 1024, 1024], P('layer', 'strip'), may hold values from -3.140625 to 3.140625
- distance: float32 [4], P('layer'), may hold values from 1024 to 2048
- templates: bfloat16 [1024, 16], replicated, may hold values from -0.1875 to 0.1875
- send_table: int32 [8, 8, 4], P('strip', None, 'layer'), may hold values from 0 to 511, as said below
- send_counts: int32 [8, 8], P('strip'), may hold values from 0 to 4, as said below
Outputs:
- pupil: bfloat16 [2, 2, 1024, 1024], P(None, None, 'strip')
- correlation: float32 [8, 8, 4, 2, 16], P('strip', None, 'layer')
The draws below stay inside these ranges and needn't reach their ends.
Inputs may be any that keep to these rules, and one draw needn't show every extreme that they name: For each source strip s the 8 x 4 entries send_table[s] are distinct subaperture numbers local to that strip (row by row over its 512 subapertures). `send_counts`: some owner receives 4 live slots from every source.
All inputs are finite; a program needn't handle non-finite values.
Results may differ from the reference program's by a relative error of at most 0.03.
Values may be sent and summed in bfloat16 or wider, within the bound.
A program may use at most 64 MiB of HBM per device.

```python
import math
import jax
import jax.numpy as jnp
from jax import lax

N = 1024
SUB = 16
CHANNELS = 16
FIELDS = 2
CAP = 4
LAYERS = 4
SIDE = 64
SUBS_DEV = 512
PIX = 1024
N_STRIP = 8


def routing_tables(key):
    base = jax.random.fold_in(key, 4177)
    order_key, count_key, owner_key = jax.random.split(base, 3)

    def shuffled(single_key):
        return jax.random.permutation(single_key, SUBS_DEV)
    orders = jax.vmap(shuffled)(jax.random.split(order_key, N_STRIP))
    table = orders[:, :N_STRIP * CAP].reshape(N_STRIP, N_STRIP, CAP).astype(jnp.int32)
    counts = jax.random.randint(count_key, (N_STRIP, N_STRIP), 0, CAP + 1, dtype=jnp.int32)
    busiest = jax.random.randint(owner_key, (), 0, N_STRIP, dtype=jnp.int32)
    counts = jnp.where(jnp.arange(N_STRIP, dtype=jnp.int32)[None, :] == busiest, CAP, counts)
    return (table, counts.astype(jnp.int32))


def draw_send_table(key, part):
    return routing_tables(key)[0]


def draw_send_counts(key, part):
    return routing_tables(key)[1]


def levels(rng, extent, shards, smallest, largest):
    def one(dim, parts):
        draws = jax.random.uniform(jax.random.fold_in(jax.random.fold_in(rng, 6), dim), (parts,), jnp.float32, smallest / len(shards), largest / len(shards))
        return jnp.repeat(jnp.exp(draws), extent[dim] // parts).reshape((-1,) + (1,) * (len(extent) - dim - 1))

    level = one(*shards[0])
    for cut in shards[1:]:
        level = level * one(*cut)
    return level


def bell_draw(rng, shape, spread, reach, shards=(), kind=jnp.bfloat16):
    loudness = levels(rng, shape, shards, -0.22, 0.18) if shards else 1.0
    entries = jax.random.normal(rng, shape, jnp.float32) * spread * loudness
    return jnp.minimum(jnp.maximum(entries, -reach), reach).astype(kind)


def setup_inputs(seed: int = 0) -> dict:
    arg_keys = jax.random.split(jax.random.key(seed), 7)
    return {
        "launch": bell_draw(arg_keys[0], (FIELDS, 2, N, N), 1.0, 6.0, ((2, 8),)),
        "screens": jnp.clip(jax.random.uniform(arg_keys[1], (LAYERS, N, N), jnp.float32, -3.140625, 3.140625), -3.140625, 3.140625),
        "distance": jnp.clip(jnp.exp(math.log(2048.0) - 0.6931472 * jax.random.uniform(arg_keys[2], (LAYERS,), jnp.float32) ** levels(arg_keys[2], (LAYERS,), ((0, 4),), -0.2, 0.2)), 1024.0, 2048.0),
        "templates": bell_draw(arg_keys[3], (PIX, CHANNELS), PIX ** -0.5, 0.1875),
        "send_table": draw_send_table(jax.random.fold_in(arg_keys[6], 71), 0),
        "send_counts": draw_send_counts(jax.random.fold_in(arg_keys[6], 71), 0),
    }


def fourier_tables(length):
    counter = jnp.arange(length, dtype=jnp.int32)
    product = counter[:, None] * counter[None, :] % length
    angles = product.astype(jnp.float32) * (2.0 * math.pi / length)
    factor = 1.0 / math.sqrt(length)
    return ((jnp.cos(angles) * factor).astype(jnp.bfloat16), (jnp.sin(angles) * factor).astype(jnp.bfloat16))

def spectral_factor(distance_value, length):
    counter = jnp.arange(length, dtype=jnp.int32)
    signed = jnp.where(counter < length // 2, counter, counter - length).astype(jnp.float32)
    phases = -distance_value * math.pi * signed * signed / float(length * length)
    return (jnp.cos(phases), jnp.sin(phases))

def spot_table(subsize):
    spotsize = 2 * subsize
    outer = jnp.arange(spotsize, dtype=jnp.int32)
    inner = jnp.arange(subsize, dtype=jnp.int32)
    angles = (inner[:, None] * outer[None, :] % spotsize).astype(jnp.float32) * (2.0 * math.pi / spotsize)
    wave_re = jnp.cos(angles) / math.sqrt(subsize)
    wave_im = -jnp.sin(angles) / math.sqrt(subsize)
    kron_re = wave_re[:, None, :, None] * wave_re[None, :, None, :] - wave_im[:, None, :, None] * wave_im[None, :, None, :]
    kron_im = wave_re[:, None, :, None] * wave_im[None, :, None, :] + wave_im[:, None, :, None] * wave_re[None, :, None, :]
    kron_re = kron_re.reshape(subsize * subsize, spotsize * spotsize)
    kron_im = kron_im.reshape(subsize * subsize, spotsize * spotsize)
    upper = jnp.concatenate([kron_re, kron_im], axis=1)
    lower = jnp.concatenate([-kron_im, kron_re], axis=1)
    return jnp.concatenate([upper, lower], axis=0).astype(jnp.bfloat16)

def rounded(value):
    return lax.optimization_barrier(value.astype(jnp.bfloat16)).astype(jnp.float32)

def layer_pass(field, screen, distance_value, cosine_table, sine_table):
    real_part = field[0].astype(jnp.float32)
    imag_part = field[1].astype(jnp.float32)
    screen_cos = jnp.cos(screen)
    screen_sin = jnp.sin(screen)
    screened = rounded(jnp.stack([real_part * screen_cos - imag_part * screen_sin, real_part * screen_sin + imag_part * screen_cos]))
    factor_re, factor_im = spectral_factor(distance_value, field.shape[2])
    along_cos = jnp.einsum('prj,jk->prk', screened, cosine_table)
    along_sin = jnp.einsum('prj,jk->prk', screened, sine_table)
    freq_re = along_cos[0] + along_sin[1]
    freq_im = along_cos[1] - along_sin[0]
    spectrum = rounded(jnp.stack([freq_re * factor_re[None, :] - freq_im * factor_im[None, :], freq_re * factor_im[None, :] + freq_im * factor_re[None, :]]))
    row_cos = jnp.einsum('pjc,jk->pkc', spectrum, cosine_table)
    row_sin = jnp.einsum('pjc,jk->pkc', spectrum, sine_table)
    wave_re = row_cos[0] + row_sin[1]
    wave_im = row_cos[1] - row_sin[0]
    phased = rounded(jnp.stack([wave_re * factor_re[:, None] - wave_im * factor_im[:, None], wave_re * factor_im[:, None] + wave_im * factor_re[:, None]]))
    back_cos = jnp.einsum('pjc,jk->pkc', phased, cosine_table)
    back_sin = jnp.einsum('pjc,jk->pkc', phased, sine_table)
    returned = rounded(jnp.stack([back_cos[0] - back_sin[1], back_cos[1] + back_sin[0]]))
    final_cos = jnp.einsum('prk,kj->prj', returned, cosine_table)
    final_sin = jnp.einsum('prk,kj->prj', returned, sine_table)
    return jnp.stack([final_cos[0] - final_sin[1], final_cos[1] + final_sin[0]]).astype(jnp.bfloat16)

def correlate_slots(slots, big_table, templates):
    pixels = templates.shape[0]
    fields_count = slots.shape[-1] // big_table.shape[0]
    shaped = slots.reshape(slots.shape[:-1] + (fields_count, big_table.shape[0])).astype(jnp.float32)
    spot_field = jnp.einsum('...i,io->...o', shaped, big_table.astype(jnp.float32))
    intensity = spot_field[..., :pixels] * spot_field[..., :pixels] + spot_field[..., pixels:] * spot_field[..., pixels:]
    intensity = rounded(intensity)
    return jnp.einsum('...i,io->...o', intensity, templates.astype(jnp.float32))

def reference(launch, screens, distance, templates, send_table, send_counts):
    cosine_bf, sine_bf = fourier_tables(N)
    cosine_table = cosine_bf.astype(jnp.float32)
    sine_table = sine_bf.astype(jnp.float32)
    finished = []
    for field_index in range(FIELDS):
        current = launch[field_index]
        for layer_index in range(LAYERS):
            current = layer_pass(current, screens[layer_index], distance[layer_index], cosine_table, sine_table)
        finished.append(current)
    pupil = jnp.stack(finished)
    blocks = pupil.reshape(FIELDS, 2, SIDE, SUB, SIDE, SUB).transpose(2, 4, 0, 1, 3, 5)
    blocks = blocks.reshape(SIDE * SIDE, FIELDS * 2 * SUB * SUB)
    offsets = (jnp.arange(N_STRIP, dtype=jnp.int32) * SUBS_DEV)[:, None, None]
    chosen = (send_table + offsets).astype(jnp.int32).reshape(-1)
    gathered = blocks[chosen].reshape(N_STRIP, N_STRIP, CAP, FIELDS * 2 * SUB * SUB)
    live = jnp.arange(CAP, dtype=jnp.int32)[None, None, :] < send_counts[:, :, None]
    gathered = jnp.where(live[:, :, :, None], gathered, jnp.zeros((), jnp.bfloat16))
    big_table = spot_table(SUB)
    correlation = correlate_slots(gathered, big_table, templates)
    return (pupil, correlation.transpose(1, 0, 2, 3, 4))
```

```python
import functools
import math

import jax
import jax.numpy as jnp
import numpy as np
from jax import lax
from jax.experimental import pallas as pl
from jax.experimental.pallas import tpu as pltpu
from jax.sharding import PartitionSpec as P

SUB = 16
F32 = jnp.float32
BF16 = jnp.bfloat16
MESH = pl.DeviceIdType.MESH


def cosine_half_table(length):
    k = np.arange(length // 2, dtype=np.int64)
    n = np.arange(length, dtype=np.int64)
    p = (k[:, None] * n[None, :]) % length
    p = np.minimum(p, length - p)
    return np.cos(2.0 * np.pi * p / length).astype(np.float32).astype(BF16)


def spot_table(subsize):
    spotsize = 2 * subsize
    outer = np.arange(spotsize)
    inner = np.arange(subsize)
    angles = (inner[:, None] * outer[None, :] % spotsize) * (2.0 * np.pi / spotsize)
    wave = (np.cos(angles) - 1j * np.sin(angles)) / math.sqrt(subsize)
    kron = wave[:, None, :, None] * wave[None, :, None, :]
    kron = kron.reshape(subsize * subsize, spotsize * spotsize)
    upper = np.concatenate([kron.real, kron.imag], axis=1)
    lower = np.concatenate([-kron.imag, kron.real], axis=1)
    return np.concatenate([upper, lower], axis=0).astype(np.float32).astype(BF16)


def kernel_line(distance_value, length):
    half = length // 2
    counter = jnp.arange(half + 1, dtype=jnp.int32).astype(F32)
    phases = -distance_value * math.pi * counter * counter / float(length * length)
    h = jnp.stack([jnp.cos(phases), jnp.sin(phases)])
    weight = jnp.where(counter == 0.0, 1.0, 2.0) / length
    folded = (h * weight)[:, :half]
    high = folded.astype(BF16)
    low = (folded - high.astype(F32)).astype(BF16)
    table = jnp.asarray(cosine_half_table(length))
    parts = jnp.dot(jnp.concatenate([high, low]), table, preferred_element_type=F32)
    sign = (1 - 2 * (jnp.arange(length, dtype=jnp.int32) % 2)).astype(F32) / length
    line = parts[:2] + parts[2:] + h[:, half:] * sign
    return jnp.concatenate([line, jnp.zeros((6, length), F32)])


def sincos(x):
    y = 0.5 * x
    z = y * y
    s = -1.0 / 39916800.0
    for c in (1.0 / 362880.0, -1.0 / 5040.0, 1.0 / 120.0, -1.0 / 6.0, 1.0):
        s = s * z + c
    s = s * y
    c0 = 1.0 / 479001600.0
    for c in (-1.0 / 3628800.0, 1.0 / 40320.0, -1.0 / 720.0, 1.0 / 24.0, -0.5, 1.0):
        c0 = c0 * z + c
    return 2.0 * s * c0, 1.0 - 2.0 * s * s


def propagate_kernel(
    layers, strips, launch_ref, scr_ref, scrt_ref, g_ref, out_ref,
    gall, gmat, early_row, early_col, stage_row, stage_col, srow, scol, sendbuf, recvbuf, slab, swapped, mid,
    gsend, grecv, ssend, srecv, xsend, xrecv, osend, orecv,
):
    count = layers * strips
    length = launch_ref.shape[-1]
    lines = launch_ref.shape[-2]
    wide = 4 * lines
    sec = lax.axis_index("layer")
    strip = lax.axis_index("strip")
    me = strip * layers + sec

    barrier = pltpu.get_barrier_semaphore()

    def greet(k, _):
        peer = lax.rem(me + k, count)
        pl.semaphore_signal(
            barrier, inc=1, device_id=(lax.rem(peer, layers), peer // layers), device_id_type=MESH
        )
        return 0

    lax.fori_loop(1, count, greet, 0)
    pl.semaphore_wait(barrier, count - 1)

    def remote(src, dst, ssem, rsem, a, s):
        return pltpu.make_async_remote_copy(
            src_ref=src, dst_ref=dst, send_sem=ssem, recv_sem=rsem,
            device_id=(a, s), device_id_type=MESH,
        )

    for k in range(1, layers):
        a = lax.rem(sec + k, layers)
        remote(g_ref, gall.at[sec], gsend, grecv.at[sec], a, strip).start()
    def to_all(start_one):
        def one(k, _):
            peer = lax.rem(me + k, count)
            start_one(lax.rem(peer, layers), peer // layers)
            return 0

        lax.fori_loop(1, count, one, 0)

    rows_of = [(stage_row, early_row)] + [(scr_ref, srow.at[i]) for i in range(layers // 2 - 1)]
    cols_of = [(stage_col, early_col)] + [(scrt_ref, scol.at[i]) for i in range(layers // 2 - 1)]

    def share(lay):
        @pl.when(sec == lay)
        def _():
            if lay % 2 == 0:
                src, dst = rows_of[lay // 2]
                if lay < 2:
                    src[...] = scr_ref[...].astype(BF16)
                for k in range(1, layers):
                    a = lax.rem(sec + k, layers)
                    remote(src.at[a], dst, ssend, srecv.at[lay], a, strip).start()
                dst[...] = src[lay]
            else:
                src, dst = cols_of[lay // 2]
                if lay < 2:
                    src[...] = scrt_ref[...].astype(BF16)

                def one(a, s):
                    remote(
                        src.at[s * layers + a], dst.at[strip], ssend, srecv.at[lay], a, s
                    ).start()

                to_all(one)
                dst[strip] = src[me]

    for lay in range(layers):
        share(lay)
    gall[sec] = g_ref[...]

    def build(lay):
        @pl.when(sec != lay)
        def _():
            remote(g_ref, gall.at[lay], gsend, grecv.at[lay], sec, strip).wait_recv()

        band = 128
        for part in range(2):
            row = gall[lay, part:part + 1, :]
            base = pltpu.roll(
                jnp.broadcast_to(row, (band, length)), 0, axis=1, stride=1, stride_axis=0
            ).astype(BF16)
            for b in range(length // band):
                at = band * b
                if b:
                    gmat[lay, part, at:at + band, 0:at] = base[:, length - at:]
                gmat[lay, part, at:at + band, at:] = base[:, :length - at]

    def screen_of(lay):
        if lay % 2 == 0:
            src, dst = rows_of[lay // 2]

            @pl.when(sec != lay)
            def _():
                remote(src.at[0], dst, ssend, srecv.at[lay], sec, strip).wait_recv()
            return sincos(dst[...].astype(F32))

        dst = cols_of[lay // 2][1]

        @pl.when(sec != lay)
        def _():
            remote(dst, dst, ssend, srecv.at[lay], sec, strip).wait_recv()

        @pl.when(sec == lay)
        def _():
            most = dst.at[pl.ds(0, strips - 1)]
            remote(most, most, ssend, srecv.at[lay], sec, strip).wait_recv()

        return sincos(jnp.concatenate([dst[s].astype(F32) for s in range(strips)], axis=1))

    def put(fc, value):
        rounded = value.astype(BF16)
        slab[fc * lines:(fc + 1) * lines, :] = rounded
        other = fc ^ 1
        swapped[other * lines:(other + 1) * lines, :] = rounded if fc % 2 == 0 else -rounded

    def screened(lay, load):
        sine, cosine = screen_of(lay)
        for f in range(2):
            re = load(2 * f)
            im = load(2 * f + 1)
            put(2 * f, re * cosine - im * sine)
            put(2 * f + 1, re * sine + im * cosine)

    block = 256

    def across(lay, step):
        per = block // lines

        def body(i, _):
            b = lax.rem(me // per + 1 + i, length // block)
            at = pl.ds(pl.multiple_of(b * block, block), block)
            dims = (((1,), (1,)), ((), ()))
            total = lax.dot_general(
                gmat[lay, 0, at, :], slab[...], dims, preferred_element_type=F32
            ) + lax.dot_general(
                gmat[lay, 1, at, :], swapped[...], dims, preferred_element_type=F32
            )
            sendbuf[step, pl.ds(b * per, per)] = total.reshape(per, lines, wide).astype(BF16)

            def one(j, _):
                peer = b * per + lax.rem(me + j, per)

                @pl.when(peer != me)
                def _():
                    remote(
                        sendbuf.at[step, peer], recvbuf.at[step, me], xsend.at[step],
                        xrecv.at[step], lax.rem(peer, layers), peer // layers,
                    ).start()
                return 0

            lax.fori_loop(0, per, one, 0)
            return 0

        lax.fori_loop(0, length // block, body, 0)

        recvbuf[step, me] = sendbuf[step, me]

    def arrived(step):
        most = recvbuf.at[step, pl.ds(0, count - 1)]
        remote(most, most, xsend.at[step], xrecv.at[step], sec, strip).wait_recv()
        if wide == 128:
            lane = lax.broadcasted_iota(jnp.int32, (lines, wide), 1) // lines
            for g in range(count // 4):
                pieces = [recvbuf[step, 4 * g + q].astype(F32) for q in range(4)]
                for fc in range(4):
                    out = None
                    for q in range(4):
                        shift = ((q - fc) * lines) % wide
                        moved = pltpu.roll(pieces[q], shift, axis=1) if shift else pieces[q]
                        out = moved if out is None else jnp.where(lane == q, moved, out)
                    rounded = out.astype(BF16)
                    at = slice(g * wide, (g + 1) * wide)
                    slab[fc * lines:(fc + 1) * lines, at] = rounded
                    other = fc ^ 1
                    swapped[other * lines:(other + 1) * lines, at] = (
                        rounded if fc % 2 == 0 else -rounded
                    )
        else:
            for fc in range(4):
                put(fc, jnp.concatenate(
                    [
                        recvbuf[step, d].astype(F32)[:, fc * lines:(fc + 1) * lines]
                        for d in range(count)
                    ],
                    axis=1,
                ))

    def along(lay):
        def body(b, _):
            at = pl.ds(pl.multiple_of(b * block, block), block)
            mid[:, at] = jnp.dot(
                slab[...], gmat[lay, 0, :, at], preferred_element_type=F32
            ) + jnp.dot(swapped[...], gmat[lay, 1, :, at], preferred_element_type=F32)
            return 0

        lax.fori_loop(0, length // block, body, 0)

    build(0)
    screened(0, lambda fc: launch_ref[fc, sec].astype(F32))
    across(0, 0)
    for lay in range(1, layers):
        build(lay)
    for lay in range(1, layers):
        arrived(lay - 1)
        along(lay - 1)
        screened(lay, lambda fc: mid[fc * lines:(fc + 1) * lines, :])
        across(lay, lay)
    arrived(layers - 1)
    along(layers - 1)
    for fc in range(4):
        out_ref[sec, fc] = mid[fc * lines:(fc + 1) * lines, :].astype(BF16)
    for k in range(1, layers):
        a = lax.rem(sec + k, layers)
        remote(out_ref.at[sec], out_ref.at[sec], osend, orecv, a, strip).start()
    most = out_ref.at[pl.ds(0, layers - 1)]
    remote(most, most, osend, orecv, sec, strip).wait()
    for k in range(1, layers):
        remote(g_ref, gall.at[sec], gsend, grecv.at[sec], sec, strip).wait_send()
    for lay in range(layers):
        @pl.when(sec == lay)
        def _(lay=lay):
            if lay % 2 == 0:
                some = rows_of[lay // 2][0].at[pl.ds(0, layers - 1)]
            else:
                some = cols_of[lay // 2][0].at[pl.ds(0, count - 1)]
            remote(some, some, ssend, srecv.at[lay], sec, strip).wait_send()
    for step in range(layers):
        most = sendbuf.at[step, pl.ds(0, count - 1)]
        remote(most, most, xsend.at[step], xrecv.at[step], sec, strip).wait_send()


def propagate(launch, screens, line, layers, strips):
    rows, length = launch.shape[2:]
    lines = rows // layers
    count = layers * strips
    vmem = pl.BlockSpec(memory_space=pltpu.VMEM)
    dma = pltpu.SemaphoreType.DMA
    screen = screens[0]
    return pl.pallas_call(
        functools.partial(propagate_kernel, layers, strips),
        out_shape=jax.ShapeDtypeStruct((layers, 4, lines, length), BF16),
        in_specs=[vmem] * 4,
        out_specs=vmem,
        scratch_shapes=[
            pltpu.VMEM((layers, 8, length), F32),
            pltpu.VMEM((layers, 2, length, length), BF16),
            pltpu.VMEM((lines, length), BF16),
            pltpu.VMEM((strips, lines, rows), BF16),
            pltpu.VMEM((layers, lines, length), BF16),
            pltpu.VMEM((count, lines, rows), BF16),
            pltpu.VMEM((layers // 2 - 1, lines, length), F32),
            pltpu.VMEM((layers // 2 - 1, strips, lines, rows), F32),
            pltpu.VMEM((layers, count, lines, 4 * lines), BF16),
            pltpu.VMEM((layers, count, lines, 4 * lines), BF16),
            pltpu.VMEM((4 * lines, length), BF16),
            pltpu.VMEM((4 * lines, length), BF16),
            pltpu.VMEM((4 * lines, length), F32),
            dma, dma((layers,)), dma, dma((layers,)), dma((layers,)), dma((layers,)), dma, dma,
        ],
        compiler_params=pltpu.CompilerParams(
            collective_id=0, has_side_effects=True, vmem_limit_bytes=56 << 20
        ),
        name="propagate",
    )(
        launch.reshape(4, layers, lines, length),
        screen.reshape(layers, lines, length),
        screen.T.reshape(count, lines, rows),
        line,
    )


def gather_kernel(side, picks_ref, pupil_ref, out_ref):
    for o in range(out_ref.shape[0]):
        pick = picks_ref[o]
        top = pl.multiple_of(pick // side * SUB, SUB)
        left = pick % side * SUB
        tile = pl.multiple_of(left // 128 * 128, 128)
        shift = (128 - left % 128) % 128
        for part in range(4):
            rows = pupil_ref[part, pl.ds(top, SUB), pl.ds(tile, 128)].astype(F32)
            out_ref[o, part] = pltpu.roll(rows, shift, axis=1)[:, :SUB].astype(BF16)


def gather_blocks(pupil, picks):
    vmem = pl.BlockSpec(memory_space=pltpu.VMEM)
    return pl.pallas_call(
        functools.partial(gather_kernel, pupil.shape[-1] // SUB),
        out_shape=jax.ShapeDtypeStruct((picks.shape[0], 4, SUB, SUB), BF16),
        in_specs=[pl.BlockSpec(memory_space=pltpu.SMEM), vmem],
        out_specs=vmem,
        name="gather",
    )(picks, pupil)


def swap_kernel(strips, in_ref, out_ref, send, recv):
    sec = lax.axis_index("layer")
    strip = lax.axis_index("strip")
    barrier = pltpu.get_barrier_semaphore()
    for k in range(1, strips):
        pl.semaphore_signal(
            barrier, inc=1, device_id=(sec, lax.rem(strip + k, strips)), device_id_type=MESH
        )
    pl.semaphore_wait(barrier, strips - 1)
    for k in range(1, strips):
        peer = lax.rem(strip + k, strips)
        pltpu.make_async_remote_copy(
            src_ref=in_ref.at[peer], dst_ref=out_ref.at[strip], send_sem=send, recv_sem=recv,
            device_id=(sec, peer), device_id_type=MESH,
        ).start()
    out_ref[strip] = in_ref[strip]
    most = out_ref.at[pl.ds(0, strips - 1)]
    pltpu.make_async_remote_copy(
        src_ref=most, dst_ref=most, send_sem=send, recv_sem=recv,
        device_id=(sec, strip), device_id_type=MESH,
    ).wait()


def swap_strips(result, strips):
    fields, channels = result.shape[1:]
    vmem = pl.BlockSpec(memory_space=pltpu.VMEM)
    dma = pltpu.SemaphoreType.DMA
    out = pl.pallas_call(
        functools.partial(swap_kernel, strips),
        out_shape=jax.ShapeDtypeStruct((strips, 8, 128), F32),
        in_specs=[vmem],
        out_specs=vmem,
        scratch_shapes=[dma, dma],
        compiler_params=pltpu.CompilerParams(collective_id=1, has_side_effects=True),
        name="swap",
    )(jnp.pad(result, ((0, 0), (0, 8 - fields), (0, 128 - channels))))
    return out[:, :fields, :channels]


QUARTER = 256
TILE = 128
PIECE = 16


def spot_rows(subsize):
    table = np.asarray(spot_table(subsize))
    split = table.reshape(2, subsize, subsize // 4, 2, 2, table.shape[1])
    return split.transpose(2, 3, 0, 4, 1, 5).reshape(table.shape)


def spread(x):
    (r0, i0), (r1, i1), (r2, i2), (r3, i3) = x
    er, ei, fr, fi = r0 + r2, i0 + i2, r1 + r3, i1 + i3
    gr, gi, dr, di = r0 - r2, i0 - i2, r1 - r3, i1 - i3
    return [(er + fr, ei + fi), (gr - di, gi + dr), (er - fr, ei - fi), (gr + di, gi - dr)]


def collect(y):
    (r0, i0), (r1, i1), (r2, i2), (r3, i3) = y
    er, ei, fr, fi = r0 + r2, i0 + i2, r1 + r3, i1 + i3
    gr, gi, dr, di = r0 - r2, i0 - i2, r1 - r3, i1 - i3
    return [(er + fr, ei + fi), (gr + di, gi - dr), (er - fr, ei - fi), (gr - di, gi + dr)]


def fused_kernel(
    info_ref, templates_ref, launch_ref, screen_ref, cosine_ref, spot_ref, out_ref, corr_ref,
    field, screen, cosine, spot, infos, lines_ref, gmat, stage, staget, screen0, columns, screen2,
    sincos_ref, slab, swapped, ybuf, send1, recv1, send2, recv2, send3, recv3, send4, recv4,
    mine, select, flat, results, answers,
    lsem, isend, irecv, ssend, srecv, xsend, xrecv, osend, orecv, csend, crecv,
):
    layers, strips, count = 4, 8, 32
    group = count // 2
    sec = lax.axis_index("layer")
    strip = lax.axis_index("strip")
    me = strip * layers + sec
    half = me // group
    place = lax.rem(me, group)

    screen1, screen3 = columns.at[pl.ds(0, strips)], columns.at[pl.ds(strips, strips)]

    copies = [
        pltpu.make_async_copy(screen_ref, screen, lsem.at[0]),
        pltpu.make_async_copy(launch_ref.at[:, sec], field, lsem.at[1]),
        pltpu.make_async_copy(cosine_ref, cosine, lsem.at[2]),
        pltpu.make_async_copy(spot_ref, spot, lsem.at[3]),
    ]
    for copy in copies:
        copy.start()

    barrier = pltpu.get_barrier_semaphore()

    def greet(k, _):
        peer = lax.rem(me + k, count)
        pl.semaphore_signal(
            barrier, inc=1, device_id=(lax.rem(peer, layers), peer // layers), device_id_type=MESH
        )
        return 0

    lax.fori_loop(1, count, greet, 0)

    def remote(src, dst, ssem, rsem, dev):
        return pltpu.make_async_remote_copy(
            src_ref=src, dst_ref=dst, send_sem=ssem, recv_sem=rsem,
            device_id=(lax.rem(dev, layers), dev // layers), device_id_type=MESH,
        )

    results[...] = jnp.zeros_like(results)
    infos[sec] = info_ref[...]
    copies[0].wait()

    @pl.when(lax.rem(sec, 2) == 0)
    def _():
        stage[...] = screen[...].astype(BF16)

    @pl.when(lax.rem(sec, 2) == 1)
    def _():
        staget[...] = screen[...].T.astype(BF16)

    pl.semaphore_wait(barrier, count - 1)

    for k in range(1, layers):
        peer = strip * layers + lax.rem(sec + k, layers)
        remote(info_ref, infos.at[sec], isend, irecv, peer).start()

    @pl.when(sec == 0)
    def _():
        for k in range(1, layers):
            remote(
                stage.at[pl.ds(32 * k, 32)], screen0, ssend, srecv.at[0], strip * layers + k
            ).start()
        screen0[...] = stage[0:32, :]

    def share_columns(dst, sem):
        def one(k, _):
            peer = lax.rem(me + k, count)
            remote(
                staget.at[pl.ds(pl.multiple_of(64 * lax.rem(peer, group), 64), 64)],
                dst.at[strip], ssend, sem, peer,
            ).start()
            return 0

        lax.fori_loop(1, count, one, 0)
        dst[strip] = staget[pl.ds(pl.multiple_of(64 * place, 64), 64), :]

    @pl.when(sec == 1)
    def _():
        share_columns(screen1, srecv.at[1])

    @pl.when(sec == 2)
    def _():
        for k in range(4):
            peer = group * (k // 2) + 2 * strip + k % 2
            src = stage.at[pl.ds(64 * (k % 2), 64)]

            @pl.when(peer != me)
            def _(peer=peer, src=src):
                remote(src, screen2, ssend, srecv.at[2], peer).start()

            @pl.when(peer == me)
            def _(src=src):
                screen2[...] = src[...]

    @pl.when(sec == 3)
    def _():
        share_columns(screen3, srecv.at[3])

    most = infos.at[pl.ds(0, layers - 1)]
    remote(most, most, isend, irecv, me).wait_recv()
    copies[2].wait()

    row8 = lax.broadcasted_iota(jnp.int32, (8, TILE), 0)
    dist = infos[3, 8:16, :]
    for lay in range(3):
        dist = jnp.where(row8 // 2 == lay, infos[lay, 8:16, :], dist)
    wide = jnp.concatenate([dist] * 4, axis=1)
    turn = 0.5 / float(1024 * 1024)

    def wave(d, squares):
        t = d * (squares * turn)
        t = t - jnp.round(t)
        sine, cosine_ = sincos(t * (-2.0 * math.pi))
        row = lax.broadcasted_iota(jnp.int32, d.shape, 0)
        return jnp.where(row % 2 == 0, cosine_, sine)

    k = lax.broadcasted_iota(jnp.int32, (8, 512), 1).astype(F32)
    weight = jnp.where(k == 0.0, 0.25, 0.5) / 1024.0
    folded = wave(wide, k * k) * weight
    high = folded.astype(BF16)
    low = (folded - high.astype(F32)).astype(BF16)
    parts = jnp.dot(
        jnp.concatenate([high.astype(F32), low.astype(F32)], axis=0).astype(BF16),
        cosine[...], preferred_element_type=F32,
    )
    last = wave(dist, jnp.full((8, TILE), 512.0 * 512.0, F32)) * (0.25 / 1024.0)
    lane8 = lax.broadcasted_iota(jnp.int32, (8, TILE), 1)
    last = jnp.where(lane8 % 2 == 0, last, -last)
    lines_ref[...] = parts[:8] + parts[8:] + jnp.concatenate([last] * 8, axis=1)

    def build(lay):
        quarters = []
        for q in range(4):
            at = slice(QUARTER * q, QUARTER * (q + 1))
            quarters.append((
                lines_ref[2 * lay:2 * lay + 1, at], lines_ref[2 * lay + 1:2 * lay + 2, at]
            ))
        for b, (re, im) in enumerate(spread(quarters)):
            turned = [(re, im), (-im, re), (-re, -im), (im, -re)][b]
            for part, (first, second) in enumerate([(turned[0], re), (turned[1], im)]):
                row = jnp.concatenate([first, second], axis=1)
                base = pltpu.roll(
                    jnp.broadcast_to(row, (TILE, 2 * QUARTER)), 0, axis=1, stride=1, stride_axis=0
                ).astype(BF16)
                gmat[lay, b, part, 0:TILE, :] = base[:, 2 * TILE:4 * TILE]
                gmat[lay, b, part, TILE:2 * TILE, :] = base[:, TILE:3 * TILE]

    def angles(lay):
        if lay == 0:
            @pl.when(sec != 0)
            def _():
                remote(screen0, screen0, ssend, srecv.at[0], me).wait_recv()

            for r in range(0, 32, PIECE):
                sine, cosine_ = sincos(screen0[r:r + PIECE, :].astype(F32))
                sincos_ref[0, r:r + PIECE, :] = sine
                sincos_ref[1, r:r + PIECE, :] = cosine_
            return
        if lay == 2:
            own = (sec == 2) & (place // 2 == strip)

            @pl.when(jnp.logical_not(own))
            def _():
                remote(screen2, screen2, ssend, srecv.at[2], me).wait_recv()

            for r in range(0, 64, PIECE):
                sine, cosine_ = sincos(screen2[r:r + PIECE, :].astype(F32))
                sincos_ref[0, r:r + PIECE, :] = sine
                sincos_ref[1, r:r + PIECE, :] = cosine_
            return
        ref = screen1 if lay == 1 else screen3

        @pl.when(sec != lay)
        def _():
            remote(ref, ref, ssend, srecv.at[lay], me).wait_recv()

        @pl.when(sec == lay)
        def _():
            some = ref.at[pl.ds(0, strips - 1)]
            remote(some, some, ssend, srecv.at[lay], me).wait_recv()

        for s in range(strips):
            sine, cosine_ = sincos(ref[s].astype(F32))
            sincos_ref[0, :, TILE * s:TILE * (s + 1)] = sine
            sincos_ref[1, :, TILE * s:TILE * (s + 1)] = cosine_

    def put(b, re_at, im_at, c, re, im):
        lanes = slice(TILE * c, TILE * (c + 1))
        re = re.astype(BF16)
        im = im.astype(BF16)
        slab[b, re_at:re_at + PIECE, lanes] = re
        slab[b, im_at:im_at + PIECE, lanes] = im
        swapped[b, re_at:re_at + PIECE, lanes] = -im
        swapped[b, im_at:im_at + PIECE, lanes] = re

    def put_all(re_at, im_at, c, x):
        for b, (re, im) in enumerate(spread(x)):
            put(b, re_at, im_at, c, re, im)

    def pieces(split):
        if split:
            return [(r, 64 + r, r) for r in range(0, 64, PIECE)]
        return [(64 * f + r, 64 * f + 32 + r, r) for f in range(2) for r in range(0, 32, PIECE)]

    def screened(x, line, c):
        out = []
        for q, (re, im) in enumerate(x):
            lanes = slice(QUARTER * q + TILE * c, QUARTER * q + TILE * (c + 1))
            sine = sincos_ref[0, line:line + PIECE, lanes]
            cosine_ = sincos_ref[1, line:line + PIECE, lanes]
            out.append((re * cosine_ - im * sine, re * sine + im * cosine_))
        return out

    def finished(re_at, im_at, c):
        lanes = slice(TILE * c, TILE * (c + 1))
        return collect([
            (ybuf[b, re_at:re_at + PIECE, lanes], ybuf[b, im_at:im_at + PIECE, lanes])
            for b in range(4)
        ])

    def along(lay):
        for b in range(4):
            ybuf[b] = jnp.dot(
                slab[b], gmat[lay, b, 0], preferred_element_type=F32
            ) + jnp.dot(swapped[b], gmat[lay, b, 1], preferred_element_type=F32)

    lane = lax.broadcasted_iota(jnp.int32, (32, TILE), 1)
    lower = lane < 64

    def across(lay, store, targets, send, recv, slot, step):
        dims = (((1,), (1,)), ((), ()))
        for chunk in range(2):
            at = slice(TILE * chunk, TILE * (chunk + 1))
            y = [
                lax.dot_general(
                    gmat[lay, (4 - b) % 4, 0, at, :], slab[b], dims, preferred_element_type=F32
                ) + lax.dot_general(
                    gmat[lay, (4 - b) % 4, 1, at, :], swapped[b], dims, preferred_element_type=F32
                )
                for b in range(4)
            ]
            for r in range(0, TILE, 32):
                y0, y1, y2, y3 = [v[r:r + 32, :] for v in y]
                even, odd, both, gap = y0 + y2, y0 - y2, y1 + y3, y1 - y3
                if step == 0:
                    turned = jnp.where(
                        lane % 64 < 32, -pltpu.roll(gap, TILE - 32, axis=1), pltpu.roll(gap, 32, axis=1)
                    )
                else:
                    moved = pltpu.roll(gap, 64, axis=1)
                    turned = jnp.where(lower, -moved, moved)
                for q, v in enumerate([even + both, odd - turned, even - both, odd + turned]):
                    store(q, chunk, r, v)

            def one(i, _, chunk=chunk):
                dev, index = targets(lax.rem(i + me, 16 if step in (0, 3) else 8), chunk)

                @pl.when(dev != me)
                def _():
                    remote(
                        send.at[index], recv.at[slot], xsend.at[step], xrecv.at[step], dev
                    ).start()
                return 0

            lax.fori_loop(0, 16 if step in (0, 3) else 8, one, 0)

    held = {}

    def store_first(q, chunk, r, v):
        p = 4 * q + 2 * chunk + r // 64
        if r % 64 == 0:
            held[q] = v
            return
        top, bottom = held[q], v
        send1[p] = jnp.where(lower, top, pltpu.roll(bottom, 64, axis=1)).astype(BF16)
        send1[group + p] = jnp.where(lower, pltpu.roll(top, 64, axis=1), bottom).astype(BF16)

    def targets_first(i, chunk):
        dev = group * (i // 8) + 4 * lax.rem(i // 2, 4) + 2 * chunk + lax.rem(i, 2)
        return dev, dev

    def store_middle(send):
        def store(q, chunk, r, v):
            send[4 * q + 2 * chunk + r // 64, r % 64:r % 64 + 32, :] = v.astype(BF16)
        return store

    def targets_middle(i, chunk):
        p = 4 * (i // 2) + 2 * chunk + lax.rem(i, 2)
        return group * half + p, p

    def store_last(q, chunk, r, v):
        send4[8 * q + 4 * chunk + r // 32] = v.astype(BF16)

    def targets_last(i, chunk):
        dev = 8 * (i // 4) + 4 * chunk + lax.rem(i, 4)
        return dev, dev

    def wait_arrival(recv, number, step):
        some = recv.at[pl.ds(0, number)]
        remote(some, some, xsend.at[step], xrecv.at[step], me).wait_recv()

    def arrive_first():
        recv1[me] = send1[me]
        wait_arrival(recv1, count - 1, 0)
        small = lax.broadcasted_iota(jnp.int32, (PIECE, TILE), 1) // 32
        for c in range(2):
            for r in range(0, 32, PIECE):
                tiles = []
                for q in range(4):
                    g = 2 * q + c
                    got = [recv1[4 * g + s, r:r + PIECE, :].astype(F32) for s in range(4)]
                    outs = []
                    for fc in range(4):
                        out = None
                        for s in range(4):
                            shift = ((s - fc) * 32) % TILE
                            moved = pltpu.roll(got[s], shift, axis=1) if shift else got[s]
                            out = moved if out is None else jnp.where(small == s, moved, out)
                        outs.append(out)
                    tiles.append(outs)
                for e in range(2):
                    at = 32 * e + r
                    put_all(at, 64 + at, c, [(t[2 * e], t[2 * e + 1]) for t in tiles])

    low16 = lax.broadcasted_iota(jnp.int32, (PIECE, TILE), 1) < 64

    def joined(recv, base, g, r):
        one = recv[base + 2 * g, r:r + PIECE, :].astype(F32)
        two = recv[base + 2 * g + 1, r:r + PIECE, :].astype(F32)
        return (
            jnp.where(low16, one, pltpu.roll(two, 64, axis=1)),
            jnp.where(low16, pltpu.roll(one, 64, axis=1), two),
        )

    def arrive_middle(send, recv, step):
        recv[place] = send[place]
        wait_arrival(recv, group - 1, step)
        for c in range(2):
            for r in range(0, 64, PIECE):
                put_all(r, 64 + r, c, [joined(recv, 0, 2 * q + c, r) for q in range(4)])

    def arrive_last():
        recv4[me] = send4[me]
        wait_arrival(recv4, count - 1, 3)
        for c in range(2):
            for f in range(2):
                for r in range(0, 32, PIECE):
                    put_all(
                        64 * f + r, 64 * f + 32 + r, c,
                        [joined(recv4, group * f, 2 * q + c, r) for q in range(4)],
                    )

    def rescreen():
        for c in range(2):
            for re_at, im_at, line in pieces(True):
                put_all(re_at, im_at, c, screened(finished(re_at, im_at, c), line, c))

    build(0)
    copies[1].wait()
    angles(0)
    for c in range(2):
        for n, (re_at, im_at, line) in enumerate(pieces(False)):
            f = n // 2
            x = []
            for q in range(4):
                lanes = slice(QUARTER * q + TILE * c, QUARTER * q + TILE * (c + 1))
                x.append((
                    field[2 * f, line:line + PIECE, lanes].astype(F32),
                    field[2 * f + 1, line:line + PIECE, lanes].astype(F32),
                ))
            put_all(re_at, im_at, c, screened(x, line, c))
    across(0, store_first, targets_first, send1, recv1, me, 0)

    for lay in range(1, layers):
        build(lay)
    pick = jnp.concatenate([infos[a, 0:8, :] for a in range(layers)], axis=0)
    block_row = jnp.floor(pick * (1.0 / 64.0))
    left = (pick - 64.0 * block_row) * 16.0
    low_row = block_row - (2 * sec).astype(F32)
    left = jnp.where((low_row == 0.0) | (low_row == 1.0), left, -4096.0)
    lane_f = lane.astype(F32)
    for k in range(SUB):
        for t in range(8):
            select[32 * k:32 * (k + 1), TILE * t:TILE * (t + 1)] = jnp.where(
                lane_f + float(TILE * t - k) == left, 1.0, 0.0
            ).astype(BF16)

    angles(1)
    arrive_first()
    along(0)
    rescreen()
    across(1, store_middle(send2), targets_middle, send2, recv2, place, 1)
    angles(2)
    arrive_middle(send2, recv2, 1)
    along(1)
    rescreen()
    across(2, store_middle(send3), targets_middle, send3, recv3, place, 2)
    angles(3)
    arrive_middle(send3, recv3, 2)
    along(2)
    rescreen()
    across(3, store_last, targets_last, send4, recv4, me, 3)
    arrive_last()
    along(3)
    own = pl.ds(pl.multiple_of(32 * sec, 32), 32)
    for c in range(2):
        for n, (re_at, im_at, line) in enumerate(pieces(False)):
            f = n // 2
            for q, (re, im) in enumerate(finished(re_at, im_at, c)):
                lanes = slice(QUARTER * q + TILE * c, QUARTER * q + TILE * (c + 1))
                mine[re_at:re_at + PIECE, lanes] = re.astype(BF16)
                mine[im_at:im_at + PIECE, lanes] = im.astype(BF16)
    for fc in range(4):
        out_ref[fc, own, :] = mine[32 * fc:32 * (fc + 1), :]
    for k in range(1, layers):
        peer = strip * layers + lax.rem(sec + k, layers)
        for fc in range(4):
            remote(
                out_ref.at[fc, own], out_ref.at[fc, own], osend, orecv, peer
            ).start()

    copies[3].wait()
    lane_row = lax.rem(lane // SUB, 2)
    match = lane_row.astype(F32) == low_row
    dims = (((1,), (1,)), ((), ()))
    taken = lax.dot_general(select[...], mine[...], dims, preferred_element_type=F32)
    folds = []
    for k in range(0, SUB, 2):
        x = jnp.where(match, taken[32 * k:32 * (k + 1), :], 0.0)
        x2 = jnp.where(match, taken[32 * (k + 1):32 * (k + 2), :], 0.0)
        x = x + pltpu.roll(x, TILE - SUB, axis=1)
        x2 = x2 + pltpu.roll(x2, SUB, axis=1)
        folds.append(jnp.where(lane_row == 0, x, x2))
    for m in range(4):
        c0, c1 = folds[2 * m], folds[2 * m + 1]
        lanes = slice(TILE * m, TILE * (m + 1))
        flat[0:32, lanes] = jnp.where(lower, c0, pltpu.roll(c1, 64, axis=1)).astype(BF16)
        flat[32:64, lanes] = jnp.where(lower, pltpu.roll(c0, 64, axis=1), c1).astype(BF16)
    total = jnp.zeros((64, 16), F32)
    for n in range(4):
        at = slice(256 * n, 256 * (n + 1))
        past = slice(1024 + 256 * n, 1024 + 256 * (n + 1))
        re = jnp.dot(flat[...], spot[:, at], preferred_element_type=F32)
        im = jnp.dot(flat[...], spot[:, past], preferred_element_type=F32)
        total = total + jnp.dot(
            (re * re + im * im).astype(BF16), templates_ref[at, :], preferred_element_type=F32
        )
    for f in range(2):
        results[:, f, 0:16] = total[32 * f:32 * (f + 1), :]

    def answer(i, _):
        dev = lax.rem(me + i, count)
        index = 8 * lax.rem(dev, layers) + dev // layers
        remote(results.at[index], answers.at[me], csend, crecv, dev).start()
        return 0

    lax.fori_loop(1, count, answer, 0)
    answers[me] = results[8 * sec + strip]

    most = out_ref.at[:, pl.ds(0, 96)]
    remote(most, most, osend, orecv, me).wait()
    some = answers.at[pl.ds(0, count - 1)]
    remote(some, some, csend, crecv, me).wait()
    for s in range(strips):
        block = answers[layers * s]
        for a in range(1, layers):
            block = block + answers[layers * s + a]
        corr_ref[s] = block[0:2, 0:16]

    some = infos.at[pl.ds(0, layers - 1)]
    remote(some, some, isend, irecv, me).wait_send()

    @pl.when(sec == 0)
    def _():
        some = stage.at[pl.ds(0, 96)]
        remote(some, some, ssend, srecv.at[0], me).wait_send()

    @pl.when(lax.rem(sec, 2) == 1)
    def _():
        some = columns.at[pl.ds(0, count - 1)]
        remote(some, some, ssend, srecv.at[1], me).wait_send()

    @pl.when(sec == 2)
    def _():
        own = place // 2 == strip

        @pl.when(own)
        def _():
            some = columns.at[pl.ds(0, 24)]
            remote(some, some, ssend, srecv.at[2], me).wait_send()

        @pl.when(jnp.logical_not(own))
        def _():
            remote(columns, columns, ssend, srecv.at[2], me).wait_send()

    for step, (send, number) in enumerate(
        [(send1, count), (send2, group), (send3, group), (send4, count)]
    ):
        some = send.at[pl.ds(0, number - 1)]
        remote(some, some, xsend.at[step], xrecv.at[step], me).wait_send()


def fused(launch, screens, info, templates):
    rows, length = launch.shape[2:]
    vmem = pl.BlockSpec(memory_space=pltpu.VMEM)
    anywhere = pl.BlockSpec(memory_space=pl.ANY)
    dma = pltpu.SemaphoreType.DMA

    def blocks(number, height):
        return pltpu.VMEM((number, height, TILE), BF16)

    return pl.pallas_call(
        fused_kernel,
        out_shape=(
            jax.ShapeDtypeStruct((4, rows, length), BF16),
            jax.ShapeDtypeStruct((8, 2, 16), F32),
        ),
        in_specs=[vmem, vmem, anywhere, anywhere, anywhere, anywhere],
        out_specs=(vmem, vmem),
        scratch_shapes=[
            pltpu.VMEM((4, 32, length), BF16),
            pltpu.VMEM((rows, length), F32),
            pltpu.VMEM((length // 2, length), BF16),
            pltpu.VMEM((512, 2048), BF16),
            pltpu.VMEM((4, 16, TILE), F32),
            pltpu.VMEM((8, length), F32),
            pltpu.VMEM((4, 4, 2, QUARTER, QUARTER), BF16),
            pltpu.VMEM((rows, length), BF16),
            pltpu.VMEM((length, rows), BF16),
            pltpu.VMEM((32, length), BF16),
            pltpu.VMEM((32, 64, TILE), BF16),
            pltpu.VMEM((64, length), BF16),
            pltpu.VMEM((2, 64, length), F32),
            pltpu.VMEM((4, TILE, QUARTER), BF16),
            pltpu.VMEM((4, TILE, QUARTER), BF16),
            pltpu.VMEM((4, TILE, QUARTER), F32),
            blocks(32, 32), blocks(32, 32),
            blocks(16, 64), blocks(16, 64),
            blocks(16, 64), blocks(16, 64),
            blocks(32, 32), blocks(32, 32),
            pltpu.VMEM((TILE, length), BF16),
            pltpu.VMEM((512, length), BF16),
            pltpu.VMEM((64, 512), BF16),
            pltpu.VMEM((32, 8, TILE), F32),
            pltpu.VMEM((32, 8, TILE), F32),
            dma((4,)), dma, dma, dma, dma((4,)), dma((4,)), dma((4,)), dma, dma, dma, dma,
        ],
        compiler_params=pltpu.CompilerParams(
            collective_id=2, has_side_effects=True, vmem_limit_bytes=48 << 20
        ),
        name="fused",
    )(
        info, templates, launch.reshape(4, 4, 32, length), screens[0],
        jnp.asarray(cosine_half_table(length)), jnp.asarray(spot_rows(SUB)),
    )


def per_device_fused(launch, screens, distance, templates, send_table, send_counts):
    sec = lax.axis_index("layer")
    rows, length = launch.shape[2:]
    pick = jnp.where(sec < send_counts[0], send_table[0, :, 0], -4096).astype(F32)
    info = jnp.concatenate([
        jnp.broadcast_to(pick[:, None], (8, TILE)), jnp.broadcast_to(distance[:, None], (8, TILE))
    ])
    pupil, found = fused(launch, screens, info, templates)
    return pupil.reshape(2, 2, rows, length), found[None, :, None]


def per_device(launch, screens, distance, templates, send_table, send_counts):
    layers = lax.axis_size("layer")
    strips = lax.axis_size("strip")
    sec = lax.axis_index("layer")
    fields = launch.shape[0]
    rows, length = launch.shape[2:]
    line = kernel_line(distance[0], length)
    done = propagate(launch, screens, line, layers, strips)
    pupil = done.transpose(1, 0, 2, 3).reshape(fields, 2, rows, length)
    side = length // SUB
    blocks = gather_blocks(pupil.reshape(2 * fields, rows, length), send_table.reshape(strips))
    flat = blocks.reshape(strips * fields, 2 * SUB * SUB)
    table = jnp.asarray(spot_table(SUB))
    pixels = templates.shape[0]
    spot = jnp.dot(flat, table, preferred_element_type=F32)
    intensity = (spot[:, :pixels] ** 2 + spot[:, pixels:] ** 2).astype(BF16)
    result = jnp.dot(intensity, templates, preferred_element_type=F32)
    result = result.reshape(strips, fields, templates.shape[1])
    live = sec < send_counts[0]
    result = jnp.where(live[:, None, None], result, 0.0)
    received = swap_strips(result, strips)
    return (pupil, received[None, :, None])


def solution(mesh):
    placed = (
        P(None, None, "strip", None),
        P("layer", "strip", None),
        P("layer"),
        P(),
        P("strip", None, "layer"),
        P("strip", None),
    )
    small = mesh.shape["layer"] == 4 and mesh.shape["strip"] == 8
    return jax.shard_map(
        per_device_fused if small else per_device,
        mesh=mesh,
        in_specs=placed,
        out_specs=(P(None, None, "strip", None), P("strip", None, "layer", None, None)),
        check_vma=False,
    )
```

```python
import functools
import math

import jax
import jax.numpy as jnp
import numpy as np
from jax import lax
from jax.experimental import pallas as pl
from jax.experimental.pallas import tpu as pltpu
from jax.sharding import PartitionSpec as P

SUB = 16
F32 = jnp.float32
BF16 = jnp.bfloat16
MESH = pl.DeviceIdType.MESH


def cosine_half_table(length):
    k = np.arange(length // 2, dtype=np.int64)
    n = np.arange(length, dtype=np.int64)
    p = (k[:, None] * n[None, :]) % length
    p = np.minimum(p, length - p)
    return np.cos(2.0 * np.pi * p / length).astype(np.float32).astype(BF16)


def spot_table(subsize):
    spotsize = 2 * subsize
    outer = np.arange(spotsize)
    inner = np.arange(subsize)
    angles = (inner[:, None] * outer[None, :] % spotsize) * (2.0 * np.pi / spotsize)
    wave = (np.cos(angles) - 1j * np.sin(angles)) / math.sqrt(subsize)
    kron = wave[:, None, :, None] * wave[None, :, None, :]
    kron = kron.reshape(subsize * subsize, spotsize * spotsize)
    upper = np.concatenate([kron.real, kron.imag], axis=1)
    lower = np.concatenate([-kron.imag, kron.real], axis=1)
    return np.concatenate([upper, lower], axis=0).astype(np.float32).astype(BF16)


def kernel_line(distance_value, length):
    half = length // 2
    counter = jnp.arange(half + 1, dtype=jnp.int32).astype(F32)
    phases = -distance_value * math.pi * counter * counter / float(length * length)
    h = jnp.stack([jnp.cos(phases), jnp.sin(phases)])
    weight = jnp.where(counter == 0.0, 1.0, 2.0) / length
    folded = (h * weight)[:, :half]
    high = folded.astype(BF16)
    low = (folded - high.astype(F32)).astype(BF16)
    table = jnp.asarray(cosine_half_table(length))
    parts = jnp.dot(jnp.concatenate([high, low]), table, preferred_element_type=F32)
    sign = (1 - 2 * (jnp.arange(length, dtype=jnp.int32) % 2)).astype(F32) / length
    line = parts[:2] + parts[2:] + h[:, half:] * sign
    return jnp.concatenate([line, jnp.zeros((6, length), F32)])


def sincos(x):
    y = 0.5 * x
    z = y * y
    s = -1.0 / 39916800.0
    for c in (1.0 / 362880.0, -1.0 / 5040.0, 1.0 / 120.0, -1.0 / 6.0, 1.0):
        s = s * z + c
    s = s * y
    c0 = 1.0 / 479001600.0
    for c in (-1.0 / 3628800.0, 1.0 / 40320.0, -1.0 / 720.0, 1.0 / 24.0, -0.5, 1.0):
        c0 = c0 * z + c
    return 2.0 * s * c0, 1.0 - 2.0 * s * s


def propagate_kernel(
    layers, strips, launch_ref, scr_ref, scrt_ref, g_ref, out_ref,
    gall, gmat, early_row, early_col, stage_row, stage_col, srow, scol, sendbuf, recvbuf, slab, swapped, mid,
    gsend, grecv, ssend, srecv, xsend, xrecv, osend, orecv,
):
    count = layers * strips
    length = launch_ref.shape[-1]
    lines = launch_ref.shape[-2]
    wide = 4 * lines
    sec = lax.axis_index("layer")
    strip = lax.axis_index("strip")
    me = strip * layers + sec

    barrier = pltpu.get_barrier_semaphore()

    def greet(k, _):
        peer = lax.rem(me + k, count)
        pl.semaphore_signal(
            barrier, inc=1, device_id=(lax.rem(peer, layers), peer // layers), device_id_type=MESH
        )
        return 0

    lax.fori_loop(1, count, greet, 0)
    pl.semaphore_wait(barrier, count - 1)

    def remote(src, dst, ssem, rsem, a, s):
        return pltpu.make_async_remote_copy(
            src_ref=src, dst_ref=dst, send_sem=ssem, recv_sem=rsem,
            device_id=(a, s), device_id_type=MESH,
        )

    for k in range(1, layers):
        a = lax.rem(sec + k, layers)
        remote(g_ref, gall.at[sec], gsend, grecv.at[sec], a, strip).start()
    def to_all(start_one):
        def one(k, _):
            peer = lax.rem(me + k, count)
            start_one(lax.rem(peer, layers), peer // layers)
            return 0

        lax.fori_loop(1, count, one, 0)

    rows_of = [(stage_row, early_row)] + [(scr_ref, srow.at[i]) for i in range(layers // 2 - 1)]
    cols_of = [(stage_col, early_col)] + [(scrt_ref, scol.at[i]) for i in range(layers // 2 - 1)]

    def share(lay):
        @pl.when(sec == lay)
        def _():
            if lay % 2 == 0:
                src, dst = rows_of[lay // 2]
                if lay < 2:
                    src[...] = scr_ref[...].astype(BF16)
                for k in range(1, layers):
                    a = lax.rem(sec + k, layers)
                    remote(src.at[a], dst, ssend, srecv.at[lay], a, strip).start()
                dst[...] = src[lay]
            else:
                src, dst = cols_of[lay // 2]
                if lay < 2:
                    src[...] = scrt_ref[...].astype(BF16)

                def one(a, s):
                    remote(
                        src.at[s * layers + a], dst.at[strip], ssend, srecv.at[lay], a, s
                    ).start()

                to_all(one)
                dst[strip] = src[me]

    for lay in range(layers):
        share(lay)
    gall[sec] = g_ref[...]

    def build(lay):
        @pl.when(sec != lay)
        def _():
            remote(g_ref, gall.at[lay], gsend, grecv.at[lay], sec, strip).wait_recv()

        band = 128
        for part in range(2):
            row = gall[lay, part:part + 1, :]
            base = pltpu.roll(
                jnp.broadcast_to(row, (band, length)), 0, axis=1, stride=1, stride_axis=0
            ).astype(BF16)
            for b in range(length // band):
                at = band * b
                if b:
                    gmat[lay, part, at:at + band, 0:at] = base[:, length - at:]
                gmat[lay, part, at:at + band, at:] = base[:, :length - at]

    def screen_of(lay):
        if lay % 2 == 0:
            src, dst = rows_of[lay // 2]

            @pl.when(sec != lay)
            def _():
                remote(src.at[0], dst, ssend, srecv.at[lay], sec, strip).wait_recv()
            return sincos(dst[...].astype(F32))

        dst = cols_of[lay // 2][1]

        @pl.when(sec != lay)
        def _():
            remote(dst, dst, ssend, srecv.at[lay], sec, strip).wait_recv()

        @pl.when(sec == lay)
        def _():
            most = dst.at[pl.ds(0, strips - 1)]
            remote(most, most, ssend, srecv.at[lay], sec, strip).wait_recv()

        return sincos(jnp.concatenate([dst[s].astype(F32) for s in range(strips)], axis=1))

    def put(fc, value):
        rounded = value.astype(BF16)
        slab[fc * lines:(fc + 1) * lines, :] = rounded
        other = fc ^ 1
        swapped[other * lines:(other + 1) * lines, :] = rounded if fc % 2 == 0 else -rounded

    def screened(lay, load):
        sine, cosine = screen_of(lay)
        for f in range(2):
            re = load(2 * f)
            im = load(2 * f + 1)
            put(2 * f, re * cosine - im * sine)
            put(2 * f + 1, re * sine + im * cosine)

    block = 256

    def across(lay, step):
        per = block // lines

        def body(i, _):
            b = lax.rem(me // per + 1 + i, length // block)
            at = pl.ds(pl.multiple_of(b * block, block), block)
            dims = (((1,), (1,)), ((), ()))
            total = lax.dot_general(
                gmat[lay, 0, at, :], slab[...], dims, preferred_element_type=F32
            ) + lax.dot_general(
                gmat[lay, 1, at, :], swapped[...], dims, preferred_element_type=F32
            )
            sendbuf[step, pl.ds(b * per, per)] = total.reshape(per, lines, wide).astype(BF16)

            def one(j, _):
                peer = b * per + lax.rem(me + j, per)

                @pl.when(peer != me)
                def _():
                    remote(
                        sendbuf.at[step, peer], recvbuf.at[step, me], xsend.at[step],
                        xrecv.at[step], lax.rem(peer, layers), peer // layers,
                    ).start()
                return 0

            lax.fori_loop(0, per, one, 0)
            return 0

        lax.fori_loop(0, length // block, body, 0)

        recvbuf[step, me] = sendbuf[step, me]

    def arrived(step):
        most = recvbuf.at[step, pl.ds(0, count - 1)]
        remote(most, most, xsend.at[step], xrecv.at[step], sec, strip).wait_recv()
        if wide == 128:
            lane = lax.broadcasted_iota(jnp.int32, (lines, wide), 1) // lines
            for g in range(count // 4):
                pieces = [recvbuf[step, 4 * g + q].astype(F32) for q in range(4)]
                for fc in range(4):
                    out = None
                    for q in range(4):
                        shift = ((q - fc) * lines) % wide
                        moved = pltpu.roll(pieces[q], shift, axis=1) if shift else pieces[q]
                        out = moved if out is None else jnp.where(lane == q, moved, out)
                    rounded = out.astype(BF16)
                    at = slice(g * wide, (g + 1) * wide)
                    slab[fc * lines:(fc + 1) * lines, at] = rounded
                    other = fc ^ 1
                    swapped[other * lines:(other + 1) * lines, at] = (
                        rounded if fc % 2 == 0 else -rounded
                    )
        else:
            for fc in range(4):
                put(fc, jnp.concatenate(
                    [
                        recvbuf[step, d].astype(F32)[:, fc * lines:(fc + 1) * lines]
                        for d in range(count)
                    ],
                    axis=1,
                ))

    def along(lay):
        def body(b, _):
            at = pl.ds(pl.multiple_of(b * block, block), block)
            mid[:, at] = jnp.dot(
                slab[...], gmat[lay, 0, :, at], preferred_element_type=F32
            ) + jnp.dot(swapped[...], gmat[lay, 1, :, at], preferred_element_type=F32)
            return 0

        lax.fori_loop(0, length // block, body, 0)

    build(0)
    screened(0, lambda fc: launch_ref[fc, sec].astype(F32))
    across(0, 0)
    for lay in range(1, layers):
        build(lay)
    for lay in range(1, layers):
        arrived(lay - 1)
        along(lay - 1)
        screened(lay, lambda fc: mid[fc * lines:(fc + 1) * lines, :])
        across(lay, lay)
    arrived(layers - 1)
    along(layers - 1)
    for fc in range(4):
        out_ref[sec, fc] = mid[fc * lines:(fc + 1) * lines, :].astype(BF16)
    for k in range(1, layers):
        a = lax.rem(sec + k, layers)
        remote(out_ref.at[sec], out_ref.at[sec], osend, orecv, a, strip).start()
    most = out_ref.at[pl.ds(0, layers - 1)]
    remote(most, most, osend, orecv, sec, strip).wait()
    for k in range(1, layers):
        remote(g_ref, gall.at[sec], gsend, grecv.at[sec], sec, strip).wait_send()
    for lay in range(layers):
        @pl.when(sec == lay)
        def _(lay=lay):
            if lay % 2 == 0:
                some = rows_of[lay // 2][0].at[pl.ds(0, layers - 1)]
            else:
                some = cols_of[lay // 2][0].at[pl.ds(0, count - 1)]
            remote(some, some, ssend, srecv.at[lay], sec, strip).wait_send()
    for step in range(layers):
        most = sendbuf.at[step, pl.ds(0, count - 1)]
        remote(most, most, xsend.at[step], xrecv.at[step], sec, strip).wait_send()


def propagate(launch, screens, line, layers, strips):
    rows, length = launch.shape[2:]
    lines = rows // layers
    count = layers * strips
    vmem = pl.BlockSpec(memory_space=pltpu.VMEM)
    dma = pltpu.SemaphoreType.DMA
    screen = screens[0]
    return pl.pallas_call(
        functools.partial(propagate_kernel, layers, strips),
        out_shape=jax.ShapeDtypeStruct((layers, 4, lines, length), BF16),
        in_specs=[vmem] * 4,
        out_specs=vmem,
        scratch_shapes=[
            pltpu.VMEM((layers, 8, length), F32),
            pltpu.VMEM((layers, 2, length, length), BF16),
            pltpu.VMEM((lines, length), BF16),
            pltpu.VMEM((strips, lines, rows), BF16),
            pltpu.VMEM((layers, lines, length), BF16),
            pltpu.VMEM((count, lines, rows), BF16),
            pltpu.VMEM((layers // 2 - 1, lines, length), F32),
            pltpu.VMEM((layers // 2 - 1, strips, lines, rows), F32),
            pltpu.VMEM((layers, count, lines, 4 * lines), BF16),
            pltpu.VMEM((layers, count, lines, 4 * lines), BF16),
            pltpu.VMEM((4 * lines, length), BF16),
            pltpu.VMEM((4 * lines, length), BF16),
            pltpu.VMEM((4 * lines, length), F32),
            dma, dma((layers,)), dma, dma((layers,)), dma((layers,)), dma((layers,)), dma, dma,
        ],
        compiler_params=pltpu.CompilerParams(
            collective_id=0, has_side_effects=True, vmem_limit_bytes=56 << 20
        ),
        name="propagate",
    )(
        launch.reshape(4, layers, lines, length),
        screen.reshape(layers, lines, length),
        screen.T.reshape(count, lines, rows),
        line,
    )


def gather_kernel(side, picks_ref, pupil_ref, out_ref):
    for o in range(out_ref.shape[0]):
        pick = picks_ref[o]
        top = pl.multiple_of(pick // side * SUB, SUB)
        left = pick % side * SUB
        tile = pl.multiple_of(left // 128 * 128, 128)
        shift = (128 - left % 128) % 128
        for part in range(4):
            rows = pupil_ref[part, pl.ds(top, SUB), pl.ds(tile, 128)].astype(F32)
            out_ref[o, part] = pltpu.roll(rows, shift, axis=1)[:, :SUB].astype(BF16)


def gather_blocks(pupil, picks):
    vmem = pl.BlockSpec(memory_space=pltpu.VMEM)
    return pl.pallas_call(
        functools.partial(gather_kernel, pupil.shape[-1] // SUB),
        out_shape=jax.ShapeDtypeStruct((picks.shape[0], 4, SUB, SUB), BF16),
        in_specs=[pl.BlockSpec(memory_space=pltpu.SMEM), vmem],
        out_specs=vmem,
        name="gather",
    )(picks, pupil)


def swap_kernel(strips, in_ref, out_ref, send, recv):
    sec = lax.axis_index("layer")
    strip = lax.axis_index("strip")
    barrier = pltpu.get_barrier_semaphore()
    for k in range(1, strips):
        pl.semaphore_signal(
            barrier, inc=1, device_id=(sec, lax.rem(strip + k, strips)), device_id_type=MESH
        )
    pl.semaphore_wait(barrier, strips - 1)
    for k in range(1, strips):
        peer = lax.rem(strip + k, strips)
        pltpu.make_async_remote_copy(
            src_ref=in_ref.at[peer], dst_ref=out_ref.at[strip], send_sem=send, recv_sem=recv,
            device_id=(sec, peer), device_id_type=MESH,
        ).start()
    out_ref[strip] = in_ref[strip]
    most = out_ref.at[pl.ds(0, strips - 1)]
    pltpu.make_async_remote_copy(
        src_ref=most, dst_ref=most, send_sem=send, recv_sem=recv,
        device_id=(sec, strip), device_id_type=MESH,
    ).wait()


def swap_strips(result, strips):
    fields, channels = result.shape[1:]
    vmem = pl.BlockSpec(memory_space=pltpu.VMEM)
    dma = pltpu.SemaphoreType.DMA
    out = pl.pallas_call(
        functools.partial(swap_kernel, strips),
        out_shape=jax.ShapeDtypeStruct((strips, 8, 128), F32),
        in_specs=[vmem],
        out_specs=vmem,
        scratch_shapes=[dma, dma],
        compiler_params=pltpu.CompilerParams(collective_id=1, has_side_effects=True),
        name="swap",
    )(jnp.pad(result, ((0, 0), (0, 8 - fields), (0, 128 - channels))))
    return out[:, :fields, :channels]


QUARTER = 256
TILE = 128
PIECE = 16


def spot_rows(subsize):
    table = np.asarray(spot_table(subsize))
    split = table.reshape(2, subsize, subsize // 4, 2, 2, table.shape[1])
    return split.transpose(2, 3, 0, 4, 1, 5).reshape(table.shape)


def spread(x):
    (r0, i0), (r1, i1), (r2, i2), (r3, i3) = x
    er, ei, fr, fi = r0 + r2, i0 + i2, r1 + r3, i1 + i3
    gr, gi, dr, di = r0 - r2, i0 - i2, r1 - r3, i1 - i3
    return [(er + fr, ei + fi), (gr - di, gi + dr), (er - fr, ei - fi), (gr + di, gi - dr)]


def collect(y):
    (r0, i0), (r1, i1), (r2, i2), (r3, i3) = y
    er, ei, fr, fi = r0 + r2, i0 + i2, r1 + r3, i1 + i3
    gr, gi, dr, di = r0 - r2, i0 - i2, r1 - r3, i1 - i3
    return [(er + fr, ei + fi), (gr + di, gi - dr), (er - fr, ei - fi), (gr - di, gi + dr)]


def fused_kernel(
    table_ref, counts_ref, distance_ref, templates_far, launch_ref, screen_ref, cosine_ref, spot_ref, out_ref, corr_ref,
    templates_ref, field, screen, cosine, spot, infos, lines_ref, gmat, stage, staget, screen0, columns, screen2,
    sincos_ref, slab, swapped, ybuf, send1, recv1, send2, recv2, send3, recv3, send4, recv4,
    mine, select, flat, results, answers,
    lsem, ready, isend, irecv, ssend, srecv, fsend, frecv, xsend, xrecv, osend, orecv, csend, crecv,
):
    layers, strips, count = 4, 8, 32
    group = count // 2
    sec = lax.axis_index("layer")
    strip = lax.axis_index("strip")
    me = strip * layers + sec
    half = me // group
    place = lax.rem(me, group)

    screen1, screen3 = columns.at[pl.ds(0, strips)], columns.at[pl.ds(strips, strips)]

    copies = [
        pltpu.make_async_copy(screen_ref, screen, lsem.at[0]),
        pltpu.make_async_copy(launch_ref.at[:, sec], field, lsem.at[1]),
        pltpu.make_async_copy(cosine_ref, cosine, lsem.at[2]),
        pltpu.make_async_copy(spot_ref, spot, lsem.at[3]),
        pltpu.make_async_copy(templates_far, templates_ref, lsem.at[4]),
    ]
    for copy in copies:
        copy.start()

    barrier = pltpu.get_barrier_semaphore()
    for k in range(1, layers):
        pl.semaphore_signal(
            barrier, inc=1, device_id=(lax.rem(sec + k, layers), strip), device_id_type=MESH
        )
    for k in range(1, strips):
        pl.semaphore_signal(
            barrier, inc=1, device_id=(sec, lax.rem(strip + k, strips)), device_id_type=MESH
        )

    def remote(src, dst, ssem, rsem, dev):
        return pltpu.make_async_remote_copy(
            src_ref=src, dst_ref=dst, send_sem=ssem, recv_sem=rsem,
            device_id=(lax.rem(dev, layers), dev // layers), device_id_type=MESH,
        )

    results[...] = jnp.zeros_like(results)
    row8 = lax.broadcasted_iota(jnp.int32, (8, TILE), 0)
    table = jnp.zeros((8, TILE), jnp.int32)
    live = jnp.zeros((8, TILE), jnp.int32)
    for o in range(8):
        table = jnp.where(row8 == o, jnp.full((8, TILE), table_ref[o], jnp.int32), table)
        live = jnp.where(row8 == o, jnp.full((8, TILE), counts_ref[o], jnp.int32), live)
    infos[sec, 0:8, :] = jnp.where(live > sec, table, -4096).astype(F32)
    infos[sec, 8:16, :] = jnp.full((8, TILE), distance_ref[0], F32)
    copies[0].wait()

    @pl.when(lax.rem(sec, 2) == 0)
    def _():
        stage[...] = screen[...].astype(BF16)

    @pl.when(lax.rem(sec, 2) == 1)
    def _():
        staget[...] = screen[...].T.astype(BF16)

    pl.semaphore_wait(barrier, layers + strips - 2)

    for k in range(1, layers):
        peer = strip * layers + lax.rem(sec + k, layers)
        remote(infos.at[sec], infos.at[sec], isend, irecv, peer).start()

    @pl.when(sec == 0)
    def _():
        for k in range(1, layers):
            remote(
                stage.at[pl.ds(32 * k, 32)], screen0, ssend, srecv.at[0], strip * layers + k
            ).start()
        screen0[...] = stage[0:32, :]

    for k in range(1, layers):
        pl.semaphore_signal(
            ready, inc=1, device_id=(lax.rem(sec + k, layers), strip), device_id_type=MESH
        )

    def share_columns(dst, sem):
        def one(k, _):
            other = lax.rem(place + k, group)
            remote(
                staget.at[pl.ds(pl.multiple_of(64 * other, 64), 64)],
                dst.at[strip], ssend, sem, group * half + other,
            ).start()
            return 0

        lax.fori_loop(1, group, one, 0)
        dst[strip] = staget[pl.ds(pl.multiple_of(64 * place, 64), 64), :]

    twin = group * (1 - half) + place
    near = place // 8 == half
    mine2 = (sec == 2) & (place // 2 == strip)

    def share(lay):
        @pl.when(sec == lay)
        def _():
            if lay != 2:
                share_columns(screen1 if lay == 1 else screen3, srecv.at[lay])
                return
            for k in range(2):
                peer = group * half + lax.rem(2 * strip, group) + k
                src = stage.at[pl.ds(64 * k, 64)]

                @pl.when(peer != me)
                def _(peer=peer, src=src):
                    remote(src, screen2, ssend, srecv.at[2], peer).start()

                @pl.when(peer == me)
                def _(src=src):
                    screen2[...] = src[...]

    def pass_on(lay):
        if lay == 2:
            @pl.when(near & jnp.logical_not(mine2))
            def _():
                remote(screen2, screen2, ssend, srecv.at[2], me).wait_recv()

            @pl.when(near)
            def _():
                remote(screen2, screen2, fsend.at[2], frecv.at[2], twin).start()
            return
        ref = screen1 if lay == 1 else screen3

        @pl.when(sec != lay)
        def _():
            some = ref.at[pl.ds(0, 4)]
            remote(some, some, ssend, srecv.at[lay], me).wait_recv()

        @pl.when(sec == lay)
        def _():
            some = ref.at[pl.ds(0, 3)]
            remote(some, some, ssend, srecv.at[lay], me).wait_recv()

        part = ref.at[pl.ds(4 * half, 4)]
        remote(part, part, fsend.at[lay], frecv.at[lay], twin).start()

    def passed(lay):
        if lay == 2:
            @pl.when(jnp.logical_not(near))
            def _():
                remote(screen2, screen2, fsend.at[2], frecv.at[2], me).wait_recv()
            return
        some = (screen1 if lay == 1 else screen3).at[pl.ds(0, 4)]
        remote(some, some, fsend.at[lay], frecv.at[lay], me).wait_recv()

    most = infos.at[pl.ds(0, layers - 1)]
    remote(most, most, isend, irecv, me).wait_recv()
    copies[2].wait()

    dist = infos[3, 8:16, :]
    for lay in range(3):
        dist = jnp.where(row8 // 2 == lay, infos[lay, 8:16, :], dist)
    wide = jnp.concatenate([dist] * 4, axis=1)
    turn = 0.5 / float(1024 * 1024)

    def wave(d, squares):
        t = d * (squares * turn)
        t = t - jnp.round(t)
        sine, cosine_ = sincos(t * (-2.0 * math.pi))
        row = lax.broadcasted_iota(jnp.int32, d.shape, 0)
        return jnp.where(row % 2 == 0, cosine_, sine)

    k = lax.broadcasted_iota(jnp.int32, (8, 512), 1).astype(F32)
    weight = jnp.where(k == 0.0, 0.25, 0.5) / 1024.0
    folded = wave(wide, k * k) * weight
    high = folded.astype(BF16)
    low = (folded - high.astype(F32)).astype(BF16)
    parts = jnp.dot(
        jnp.concatenate([high.astype(F32), low.astype(F32)], axis=0).astype(BF16),
        cosine[...], preferred_element_type=F32,
    )
    last = wave(dist, jnp.full((8, TILE), 512.0 * 512.0, F32)) * (0.25 / 1024.0)
    lane8 = lax.broadcasted_iota(jnp.int32, (8, TILE), 1)
    last = jnp.where(lane8 % 2 == 0, last, -last)
    lines_ref[...] = parts[:8] + parts[8:] + jnp.concatenate([last] * 8, axis=1)

    def build(lay):
        quarters = []
        for q in range(4):
            at = slice(QUARTER * q, QUARTER * (q + 1))
            quarters.append((
                lines_ref[2 * lay:2 * lay + 1, at], lines_ref[2 * lay + 1:2 * lay + 2, at]
            ))
        for b, (re, im) in enumerate(spread(quarters)):
            turned = [(re, im), (-im, re), (-re, -im), (im, -re)][b]
            for part, (first, second) in enumerate([(turned[0], re), (turned[1], im)]):
                row = jnp.concatenate([first, second], axis=1)
                base = pltpu.roll(
                    jnp.broadcast_to(row, (TILE, 2 * QUARTER)), 0, axis=1, stride=1, stride_axis=0
                ).astype(BF16)
                gmat[lay, b, part, 0:TILE, :] = base[:, 2 * TILE:4 * TILE]
                gmat[lay, b, part, TILE:2 * TILE, :] = base[:, TILE:3 * TILE]

    def angles(lay):
        if lay == 0:
            @pl.when(sec != 0)
            def _():
                remote(screen0, screen0, ssend, srecv.at[0], me).wait_recv()

            for r in range(0, 32, PIECE):
                sine, cosine_ = sincos(screen0[r:r + PIECE, :].astype(F32))
                sincos_ref[0, r:r + PIECE, :] = sine
                sincos_ref[1, r:r + PIECE, :] = cosine_
            return
        passed(lay)
        if lay == 2:
            for r in range(0, 64, PIECE):
                sine, cosine_ = sincos(screen2[r:r + PIECE, :].astype(F32))
                sincos_ref[0, r:r + PIECE, :] = sine
                sincos_ref[1, r:r + PIECE, :] = cosine_
            return
        ref = screen1 if lay == 1 else screen3
        for s in range(strips):
            sine, cosine_ = sincos(ref[s].astype(F32))
            sincos_ref[0, :, TILE * s:TILE * (s + 1)] = sine
            sincos_ref[1, :, TILE * s:TILE * (s + 1)] = cosine_

    def put(b, re_at, im_at, c, re, im):
        lanes = slice(TILE * c, TILE * (c + 1))
        re = re.astype(BF16)
        im = im.astype(BF16)
        slab[b, re_at:re_at + PIECE, lanes] = re
        slab[b, im_at:im_at + PIECE, lanes] = im
        swapped[b, re_at:re_at + PIECE, lanes] = -im
        swapped[b, im_at:im_at + PIECE, lanes] = re

    def put_all(re_at, im_at, c, x):
        for b, (re, im) in enumerate(spread(x)):
            put(b, re_at, im_at, c, re, im)

    def pieces(split):
        if split:
            return [(r, 64 + r, r) for r in range(0, 64, PIECE)]
        return [(64 * f + r, 64 * f + 32 + r, r) for f in range(2) for r in range(0, 32, PIECE)]

    def screened(x, line, c):
        out = []
        for q, (re, im) in enumerate(x):
            lanes = slice(QUARTER * q + TILE * c, QUARTER * q + TILE * (c + 1))
            sine = sincos_ref[0, line:line + PIECE, lanes]
            cosine_ = sincos_ref[1, line:line + PIECE, lanes]
            out.append((re * cosine_ - im * sine, re * sine + im * cosine_))
        return out

    def finished(re_at, im_at, c):
        lanes = slice(TILE * c, TILE * (c + 1))
        return collect([
            (ybuf[b, re_at:re_at + PIECE, lanes], ybuf[b, im_at:im_at + PIECE, lanes])
            for b in range(4)
        ])

    def along(lay, first=0, number=TILE):
        at = slice(first, first + number)
        for b in range(4):
            ybuf[b, at, :] = jnp.dot(
                slab[b, at, :], gmat[lay, b, 0], preferred_element_type=F32
            ) + jnp.dot(swapped[b, at, :], gmat[lay, b, 1], preferred_element_type=F32)

    lane = lax.broadcasted_iota(jnp.int32, (32, TILE), 1)
    lower = lane < 64

    def across(lay, store, targets, send, recv, slot, step):
        dims = (((1,), (1,)), ((), ()))
        for chunk in range(2):
            at = slice(TILE * chunk, TILE * (chunk + 1))
            y = [
                lax.dot_general(
                    gmat[lay, (4 - b) % 4, 0, at, :], slab[b], dims, preferred_element_type=F32
                ) + lax.dot_general(
                    gmat[lay, (4 - b) % 4, 1, at, :], swapped[b], dims, preferred_element_type=F32
                )
                for b in range(4)
            ]
            for r in range(0, TILE, 32):
                y0, y1, y2, y3 = [v[r:r + 32, :] for v in y]
                even, odd, both, gap = y0 + y2, y0 - y2, y1 + y3, y1 - y3
                if step == 0:
                    turned = jnp.where(
                        lane % 64 < 32, -pltpu.roll(gap, TILE - 32, axis=1), pltpu.roll(gap, 32, axis=1)
                    )
                else:
                    moved = pltpu.roll(gap, 64, axis=1)
                    turned = jnp.where(lower, -moved, moved)
                for q, v in enumerate([even + both, odd - turned, even - both, odd + turned]):
                    store(q, chunk, r, v)

            def one(i, _, chunk=chunk):
                dev, index = targets(lax.rem(i + me, 16 if step in (0, 3) else 8), chunk)

                @pl.when(dev != me)
                def _():
                    src, dst = (send.at[0], recv.at[0]) if step == 3 else (send, recv)
                    remote(
                        src.at[index], dst.at[slot], xsend.at[step], xrecv.at[step], dev
                    ).start()
                return 0

            lax.fori_loop(0, 16 if step in (0, 3) else 8, one, 0)

        if step == 3:
            def late(i, _):
                dev = lax.rem(i + me, count)
                remote(
                    send.at[1, dev], recv.at[1, me], xsend.at[4], xrecv.at[4], dev
                ).start()
                return 0

            lax.fori_loop(1, count, late, 0)

    held = {}

    def store_first(q, chunk, r, v):
        p = 4 * q + 2 * chunk + r // 64
        if r % 64 == 0:
            held[q] = v
            return
        top, bottom = held[q], v
        send1[p] = jnp.where(lower, top, pltpu.roll(bottom, 64, axis=1)).astype(BF16)
        send1[group + p] = jnp.where(lower, pltpu.roll(top, 64, axis=1), bottom).astype(BF16)

    def targets_first(i, chunk):
        dev = group * (i // 8) + 4 * lax.rem(i // 2, 4) + 2 * chunk + lax.rem(i, 2)
        return dev, dev

    def store_middle(send):
        def store(q, chunk, r, v):
            send[4 * q + 2 * chunk + r // 64, r % 64:r % 64 + 32, :] = v.astype(BF16)
        return store

    def targets_middle(i, chunk):
        p = 4 * (i // 2) + 2 * chunk + lax.rem(i, 2)
        return group * half + p, p

    def store_last(q, chunk, r, v):
        for n in range(2):
            send4[n, 8 * q + 4 * chunk + r // 32] = v[16 * n:16 * (n + 1), :].astype(BF16)

    def targets_last(i, chunk):
        dev = 8 * (i // 4) + 4 * chunk + lax.rem(i, 4)
        return dev, dev

    def wait_arrival(recv, number, step):
        some = recv.at[pl.ds(0, number)]
        remote(some, some, xsend.at[step], xrecv.at[step], me).wait_recv()

    def arrive_first():
        recv1[me] = send1[me]
        wait_arrival(recv1, count - 1, 0)
        small = lax.broadcasted_iota(jnp.int32, (PIECE, TILE), 1) // 32
        for c in range(2):
            for r in range(0, 32, PIECE):
                tiles = []
                for q in range(4):
                    g = 2 * q + c
                    got = [recv1[4 * g + s, r:r + PIECE, :].astype(F32) for s in range(4)]
                    outs = []
                    for fc in range(4):
                        out = None
                        for s in range(4):
                            shift = ((s - fc) * 32) % TILE
                            moved = pltpu.roll(got[s], shift, axis=1) if shift else got[s]
                            out = moved if out is None else jnp.where(small == s, moved, out)
                        outs.append(out)
                    tiles.append(outs)
                for e in range(2):
                    at = 32 * e + r
                    put_all(at, 64 + at, c, [(t[2 * e], t[2 * e + 1]) for t in tiles])

    low16 = lax.broadcasted_iota(jnp.int32, (PIECE, TILE), 1) < 64

    def joined(recv, base, g, r):
        one = recv[base + 2 * g, r:r + PIECE, :].astype(F32)
        two = recv[base + 2 * g + 1, r:r + PIECE, :].astype(F32)
        return (
            jnp.where(low16, one, pltpu.roll(two, 64, axis=1)),
            jnp.where(low16, pltpu.roll(one, 64, axis=1), two),
        )

    def arrive_middle(send, recv, step):
        recv[place] = send[place]
        wait_arrival(recv, group - 1, step)
        for c in range(2):
            for r in range(0, 64, PIECE):
                put_all(r, 64 + r, c, [joined(recv, 0, 2 * q + c, r) for q in range(4)])

    def arrive_last(n):
        recv, send = recv4.at[n], send4.at[n]
        recv[me] = send[me]
        wait_arrival(recv, count - 1, 3 + n)
        for c in range(2):
            for f in range(2):
                at = 64 * n + 32 * f
                put_all(
                    at, at + 16, c, [joined(recv, group * f, 2 * q + c, 0) for q in range(4)]
                )

    def rescreen():
        for c in range(2):
            for re_at, im_at, line in pieces(True):
                put_all(re_at, im_at, c, screened(finished(re_at, im_at, c), line, c))

    build(0)
    pl.semaphore_wait(ready, layers - 1)
    share(1)
    copies[1].wait()
    angles(0)
    for c in range(2):
        for n, (re_at, im_at, line) in enumerate(pieces(False)):
            f = n // 2
            x = []
            for q in range(4):
                lanes = slice(QUARTER * q + TILE * c, QUARTER * q + TILE * (c + 1))
                x.append((
                    field[2 * f, line:line + PIECE, lanes].astype(F32),
                    field[2 * f + 1, line:line + PIECE, lanes].astype(F32),
                ))
            put_all(re_at, im_at, c, screened(x, line, c))
    across(0, store_first, targets_first, send1, recv1, me, 0)

    share(2)
    share(3)
    pass_on(1)
    for lay in range(1, layers):
        build(lay)
    pick = jnp.concatenate([infos[a, 0:8, :] for a in range(layers)], axis=0)
    block_row = jnp.floor(pick * (1.0 / 64.0))
    left = (pick - 64.0 * block_row) * 16.0
    low_row = block_row - (2 * sec).astype(F32)
    left = jnp.where((low_row == 0.0) | (low_row == 1.0), left, -4096.0)
    lane_f = lane.astype(F32)
    for k in range(SUB):
        for t in range(8):
            select[32 * k:32 * (k + 1), TILE * t:TILE * (t + 1)] = jnp.where(
                lane_f + float(TILE * t - k) == left, 1.0, 0.0
            ).astype(BF16)

    angles(1)
    arrive_first()
    along(0)
    rescreen()
    across(1, store_middle(send2), targets_middle, send2, recv2, place, 1)
    pass_on(2)
    pass_on(3)
    angles(2)
    arrive_middle(send2, recv2, 1)
    along(1)
    rescreen()
    across(2, store_middle(send3), targets_middle, send3, recv3, place, 2)
    angles(3)
    arrive_middle(send3, recv3, 2)
    along(2)
    rescreen()
    across(3, store_last, targets_last, send4, recv4, me, 3)
    beside = strip * layers + sec + 1 - 2 * lax.rem(sec, 2)
    above = strip * layers + lax.rem(sec + 2, layers)

    def rows_of(n, owner):
        return pl.ds(pl.multiple_of(32 * owner + 16 * n, 16), 16)

    def publish(n):
        own = rows_of(n, sec)
        for fc in range(4):
            f, part = fc // 2, fc % 2
            out_ref[fc, own, :] = mine[64 * f + 32 * part + 16 * n:64 * f + 32 * part + 16 * n + 16, :]
        part = out_ref.at[:, own]
        remote(part, part, osend.at[4 * n], orecv.at[4 * n], beside).start()
        remote(part, part, osend.at[4 * n + 1], orecv.at[4 * n + 1], above).start()

    def relay(n):
        part = out_ref.at[:, rows_of(n, sec)]
        remote(part, part, osend.at[4 * n], orecv.at[4 * n], me).wait_recv()
        given = out_ref.at[pl.ds(0, 2), rows_of(n, sec + 1 - 2 * lax.rem(sec, 2))]
        remote(given, given, osend.at[4 * n + 2], orecv.at[4 * n + 2], above).start()
        remote(part, part, osend.at[4 * n + 1], orecv.at[4 * n + 1], me).wait_recv()
        given = out_ref.at[pl.ds(2, 2), rows_of(n, lax.rem(sec + 2, layers))]
        remote(given, given, osend.at[4 * n + 3], orecv.at[4 * n + 3], beside).start()

    for n in range(2):
        arrive_last(n)
        along(3, 64 * n, 64)
        for c in range(2):
            for f in range(2):
                at = 64 * n + 32 * f
                for q, (re, im) in enumerate(finished(at, at + 16, c)):
                    lanes = slice(QUARTER * q + TILE * c, QUARTER * q + TILE * (c + 1))
                    to = 64 * f + 16 * n
                    mine[to:to + PIECE, lanes] = re.astype(BF16)
                    mine[to + 32:to + 32 + PIECE, lanes] = im.astype(BF16)
        publish(n)
    relay(0)

    copies[3].wait()
    copies[4].wait()
    lane_row = lax.rem(lane // SUB, 2)
    match = lane_row.astype(F32) == low_row
    dims = (((1,), (1,)), ((), ()))
    taken = lax.dot_general(select[...], mine[...], dims, preferred_element_type=F32)
    folds = []
    for k in range(0, SUB, 2):
        x = jnp.where(match, taken[32 * k:32 * (k + 1), :], 0.0)
        x2 = jnp.where(match, taken[32 * (k + 1):32 * (k + 2), :], 0.0)
        x = x + pltpu.roll(x, TILE - SUB, axis=1)
        x2 = x2 + pltpu.roll(x2, SUB, axis=1)
        folds.append(jnp.where(lane_row == 0, x, x2))
    for m in range(4):
        c0, c1 = folds[2 * m], folds[2 * m + 1]
        lanes = slice(TILE * m, TILE * (m + 1))
        flat[0:32, lanes] = jnp.where(lower, c0, pltpu.roll(c1, 64, axis=1)).astype(BF16)
        flat[32:64, lanes] = jnp.where(lower, pltpu.roll(c0, 64, axis=1), c1).astype(BF16)
    total = jnp.zeros((64, 16), F32)
    for n in range(4):
        at = slice(256 * n, 256 * (n + 1))
        past = slice(1024 + 256 * n, 1024 + 256 * (n + 1))
        re = jnp.dot(flat[...], spot[:, at], preferred_element_type=F32)
        im = jnp.dot(flat[...], spot[:, past], preferred_element_type=F32)
        total = total + lax.dot_general(
            (re * re + im * im).astype(BF16), templates_ref[:, at], dims, preferred_element_type=F32
        )
    for f in range(2):
        results[:, f, 0:16] = total[32 * f:32 * (f + 1), :]

    def answer(i, _):
        dev = lax.rem(me + i, count)
        index = 8 * lax.rem(dev, layers) + dev // layers
        remote(results.at[index], answers.at[me], csend, crecv, dev).start()
        return 0

    lax.fori_loop(1, count, answer, 0)
    answers[me] = results[8 * sec + strip]

    relay(1)
    for n in range(2):
        part = out_ref.at[:, rows_of(n, sec)]
        for k in range(2):
            remote(part, part, osend.at[4 * n + k], orecv.at[4 * n + k], me).wait_send()
            given = out_ref.at[pl.ds(0, 2), rows_of(n, sec)]
            remote(given, given, osend.at[4 * n + 2 + k], orecv.at[4 * n + 2 + k], me).wait()
    some = answers.at[pl.ds(0, count - 1)]
    remote(some, some, csend, crecv, me).wait()
    for s in range(strips):
        block = answers[layers * s]
        for a in range(1, layers):
            block = block + answers[layers * s + a]
        corr_ref[s] = block[0:2, 0:16]

    some = infos.at[pl.ds(0, layers - 1)]
    remote(some, some, isend, irecv, me).wait_send()

    @pl.when(sec == 0)
    def _():
        some = stage.at[pl.ds(0, 96)]
        remote(some, some, ssend, srecv.at[0], me).wait_send()

    @pl.when(lax.rem(sec, 2) == 1)
    def _():
        some = columns.at[pl.ds(0, group - 1)]
        remote(some, some, ssend, srecv.at[1], me).wait_send()

    @pl.when((sec == 2) & mine2)
    def _():
        remote(screen2, screen2, ssend, srecv.at[2], me).wait_send()

    @pl.when((sec == 2) & jnp.logical_not(mine2))
    def _():
        remote(stage, stage, ssend, srecv.at[2], me).wait_send()

    @pl.when(near)
    def _():
        remote(screen2, screen2, fsend.at[2], frecv.at[2], me).wait_send()

    for lay, ref in ((1, screen1), (3, screen3)):
        some = ref.at[pl.ds(0, 4)]
        remote(some, some, fsend.at[lay], frecv.at[lay], me).wait_send()

    for step, (send, number) in enumerate(
        [(send1, count), (send2, group), (send3, group), (send4.at[0], count), (send4.at[1], count)]
    ):
        some = send.at[pl.ds(0, number - 1)]
        remote(some, some, xsend.at[step], xrecv.at[step], me).wait_send()


def fused(launch, screens, distance, templates, send_table, send_counts):
    rows, length = launch.shape[2:]
    vmem = pl.BlockSpec(memory_space=pltpu.VMEM)
    smem = pl.BlockSpec(memory_space=pltpu.SMEM)
    far = pl.BlockSpec(memory_space=pltpu.HBM)
    dma = pltpu.SemaphoreType.DMA

    def blocks(number, height):
        return pltpu.VMEM((number, height, TILE), BF16)

    return pl.pallas_call(
        fused_kernel,
        out_shape=(
            jax.ShapeDtypeStruct((4, rows, length), BF16),
            jax.ShapeDtypeStruct((8, 2, 16), F32),
        ),
        in_specs=[smem, smem, smem, far, far, far, far, far],
        out_specs=(vmem, vmem),
        scratch_shapes=[
            pltpu.VMEM(templates.shape[::-1], BF16),
            pltpu.VMEM((4, 32, length), BF16),
            pltpu.VMEM((rows, length), F32),
            pltpu.VMEM((length // 2, length), BF16),
            pltpu.VMEM((512, 2048), BF16),
            pltpu.VMEM((4, 16, TILE), F32),
            pltpu.VMEM((8, length), F32),
            pltpu.VMEM((4, 4, 2, QUARTER, QUARTER), BF16),
            pltpu.VMEM((rows, length), BF16),
            pltpu.VMEM((length, rows), BF16),
            pltpu.VMEM((32, length), BF16),
            pltpu.VMEM((16, 64, TILE), BF16),
            pltpu.VMEM((64, length), BF16),
            pltpu.VMEM((2, 64, length), F32),
            pltpu.VMEM((4, TILE, QUARTER), BF16),
            pltpu.VMEM((4, TILE, QUARTER), BF16),
            pltpu.VMEM((4, TILE, QUARTER), F32),
            blocks(32, 32), blocks(32, 32),
            blocks(16, 64), blocks(16, 64),
            blocks(16, 64), blocks(16, 64),
            pltpu.VMEM((2, 32, 16, TILE), BF16), pltpu.VMEM((2, 32, 16, TILE), BF16),
            pltpu.VMEM((TILE, length), BF16),
            pltpu.VMEM((512, length), BF16),
            pltpu.VMEM((64, 512), BF16),
            pltpu.VMEM((32, 2, TILE), F32),
            pltpu.VMEM((32, 2, TILE), F32),
            dma((5,)), pltpu.SemaphoreType.REGULAR, dma, dma, dma, dma((4,)), dma((4,)), dma((4,)),
            dma((5,)), dma((5,)), dma((8,)), dma((8,)), dma, dma,
        ],
        compiler_params=pltpu.CompilerParams(
            collective_id=2, has_side_effects=True, vmem_limit_bytes=60 << 20
        ),
        name="fused",
    )(
        send_table.reshape(8), send_counts.reshape(8), distance, templates.T, launch.reshape(4, 4, 32, length), screens[0],
        jnp.asarray(cosine_half_table(length)), jnp.asarray(spot_rows(SUB)),
    )


def per_device_fused(launch, screens, distance, templates, send_table, send_counts):
    rows, length = launch.shape[2:]
    pupil, found = fused(launch, screens, distance, templates, send_table, send_counts)
    return pupil.reshape(2, 2, rows, length), found[None, :, None]


def per_device(launch, screens, distance, templates, send_table, send_counts):
    layers = lax.axis_size("layer")
    strips = lax.axis_size("strip")
    sec = lax.axis_index("layer")
    fields = launch.shape[0]
    rows, length = launch.shape[2:]
    line = kernel_line(distance[0], length)
    done = propagate(launch, screens, line, layers, strips)
    pupil = done.transpose(1, 0, 2, 3).reshape(fields, 2, rows, length)
    side = length // SUB
    blocks = gather_blocks(pupil.reshape(2 * fields, rows, length), send_table.reshape(strips))
    flat = blocks.reshape(strips * fields, 2 * SUB * SUB)
    table = jnp.asarray(spot_table(SUB))
    pixels = templates.shape[0]
    spot = jnp.dot(flat, table, preferred_element_type=F32)
    intensity = (spot[:, :pixels] ** 2 + spot[:, pixels:] ** 2).astype(BF16)
    result = jnp.dot(intensity, templates, preferred_element_type=F32)
    result = result.reshape(strips, fields, templates.shape[1])
    live = sec < send_counts[0]
    result = jnp.where(live[:, None, None], result, 0.0)
    received = swap_strips(result, strips)
    return (pupil, received[None, :, None])


def solution(mesh):
    placed = (
        P(None, None, "strip", None),
        P("layer", "strip", None),
        P("layer"),
        P(),
        P("strip", None, "layer"),
        P("strip", None),
    )
    small = mesh.shape["layer"] == 4 and mesh.shape["strip"] == 8
    return jax.shard_map(
        per_device_fused if small else per_device,
        mesh=mesh,
        in_specs=placed,
        out_specs=(P(None, None, "strip", None), P("strip", None, "layer", None, None)),
        check_vma=False,
    )
```

```python
import functools
import math

import jax
import jax.numpy as jnp
import numpy as np
from jax import lax
from jax.experimental import pallas as pl
from jax.experimental.pallas import tpu as pltpu
from jax.sharding import PartitionSpec as P

SUB = 16
F32 = jnp.float32
BF16 = jnp.bfloat16
MESH = pl.DeviceIdType.MESH


def cosine_half_table(length):
    k = np.arange(length // 2, dtype=np.int64)
    n = np.arange(length, dtype=np.int64)
    p = (k[:, None] * n[None, :]) % length
    p = np.minimum(p, length - p)
    return np.cos(2.0 * np.pi * p / length).astype(np.float32).astype(BF16)


def spot_table(subsize):
    spotsize = 2 * subsize
    outer = np.arange(spotsize)
    inner = np.arange(subsize)
    angles = (inner[:, None] * outer[None, :] % spotsize) * (2.0 * np.pi / spotsize)
    wave = (np.cos(angles) - 1j * np.sin(angles)) / math.sqrt(subsize)
    kron = wave[:, None, :, None] * wave[None, :, None, :]
    kron = kron.reshape(subsize * subsize, spotsize * spotsize)
    upper = np.concatenate([kron.real, kron.imag], axis=1)
    lower = np.concatenate([-kron.imag, kron.real], axis=1)
    return np.concatenate([upper, lower], axis=0).astype(np.float32).astype(BF16)


def kernel_line(distance_value, length):
    half = length // 2
    counter = jnp.arange(half + 1, dtype=jnp.int32).astype(F32)
    phases = -distance_value * math.pi * counter * counter / float(length * length)
    h = jnp.stack([jnp.cos(phases), jnp.sin(phases)])
    weight = jnp.where(counter == 0.0, 1.0, 2.0) / length
    folded = (h * weight)[:, :half]
    high = folded.astype(BF16)
    low = (folded - high.astype(F32)).astype(BF16)
    table = jnp.asarray(cosine_half_table(length))
    parts = jnp.dot(jnp.concatenate([high, low]), table, preferred_element_type=F32)
    sign = (1 - 2 * (jnp.arange(length, dtype=jnp.int32) % 2)).astype(F32) / length
    line = parts[:2] + parts[2:] + h[:, half:] * sign
    return jnp.concatenate([line, jnp.zeros((6, length), F32)])


def sincos(x):
    y = 0.5 * x
    z = y * y
    s = -1.0 / 39916800.0
    for c in (1.0 / 362880.0, -1.0 / 5040.0, 1.0 / 120.0, -1.0 / 6.0, 1.0):
        s = s * z + c
    s = s * y
    c0 = 1.0 / 479001600.0
    for c in (-1.0 / 3628800.0, 1.0 / 40320.0, -1.0 / 720.0, 1.0 / 24.0, -0.5, 1.0):
        c0 = c0 * z + c
    return 2.0 * s * c0, 1.0 - 2.0 * s * s


def propagate_kernel(
    layers, strips, launch_ref, scr_ref, scrt_ref, g_ref, out_ref,
    gall, gmat, early_row, early_col, stage_row, stage_col, srow, scol, sendbuf, recvbuf, slab, swapped, mid,
    gsend, grecv, ssend, srecv, xsend, xrecv, osend, orecv,
):
    count = layers * strips
    length = launch_ref.shape[-1]
    lines = launch_ref.shape[-2]
    wide = 4 * lines
    sec = lax.axis_index("layer")
    strip = lax.axis_index("strip")
    me = strip * layers + sec

    barrier = pltpu.get_barrier_semaphore()

    def greet(k, _):
        peer = lax.rem(me + k, count)
        pl.semaphore_signal(
            barrier, inc=1, device_id=(lax.rem(peer, layers), peer // layers), device_id_type=MESH
        )
        return 0

    lax.fori_loop(1, count, greet, 0)
    pl.semaphore_wait(barrier, count - 1)

    def remote(src, dst, ssem, rsem, a, s):
        return pltpu.make_async_remote_copy(
            src_ref=src, dst_ref=dst, send_sem=ssem, recv_sem=rsem,
            device_id=(a, s), device_id_type=MESH,
        )

    for k in range(1, layers):
        a = lax.rem(sec + k, layers)
        remote(g_ref, gall.at[sec], gsend, grecv.at[sec], a, strip).start()
    def to_all(start_one):
        def one(k, _):
            peer = lax.rem(me + k, count)
            start_one(lax.rem(peer, layers), peer // layers)
            return 0

        lax.fori_loop(1, count, one, 0)

    rows_of = [(stage_row, early_row)] + [(scr_ref, srow.at[i]) for i in range(layers // 2 - 1)]
    cols_of = [(stage_col, early_col)] + [(scrt_ref, scol.at[i]) for i in range(layers // 2 - 1)]

    def share(lay):
        @pl.when(sec == lay)
        def _():
            if lay % 2 == 0:
                src, dst = rows_of[lay // 2]
                if lay < 2:
                    src[...] = scr_ref[...].astype(BF16)
                for k in range(1, layers):
                    a = lax.rem(sec + k, layers)
                    remote(src.at[a], dst, ssend, srecv.at[lay], a, strip).start()
                dst[...] = src[lay]
            else:
                src, dst = cols_of[lay // 2]
                if lay < 2:
                    src[...] = scrt_ref[...].astype(BF16)

                def one(a, s):
                    remote(
                        src.at[s * layers + a], dst.at[strip], ssend, srecv.at[lay], a, s
                    ).start()

                to_all(one)
                dst[strip] = src[me]

    for lay in range(layers):
        share(lay)
    gall[sec] = g_ref[...]

    def build(lay):
        @pl.when(sec != lay)
        def _():
            remote(g_ref, gall.at[lay], gsend, grecv.at[lay], sec, strip).wait_recv()

        band = 128
        for part in range(2):
            row = gall[lay, part:part + 1, :]
            base = pltpu.roll(
                jnp.broadcast_to(row, (band, length)), 0, axis=1, stride=1, stride_axis=0
            ).astype(BF16)
            for b in range(length // band):
                at = band * b
                if b:
                    gmat[lay, part, at:at + band, 0:at] = base[:, length - at:]
                gmat[lay, part, at:at + band, at:] = base[:, :length - at]

    def screen_of(lay):
        if lay % 2 == 0:
            src, dst = rows_of[lay // 2]

            @pl.when(sec != lay)
            def _():
                remote(src.at[0], dst, ssend, srecv.at[lay], sec, strip).wait_recv()
            return sincos(dst[...].astype(F32))

        dst = cols_of[lay // 2][1]

        @pl.when(sec != lay)
        def _():
            remote(dst, dst, ssend, srecv.at[lay], sec, strip).wait_recv()

        @pl.when(sec == lay)
        def _():
            most = dst.at[pl.ds(0, strips - 1)]
            remote(most, most, ssend, srecv.at[lay], sec, strip).wait_recv()

        return sincos(jnp.concatenate([dst[s].astype(F32) for s in range(strips)], axis=1))

    def put(fc, value):
        rounded = value.astype(BF16)
        slab[fc * lines:(fc + 1) * lines, :] = rounded
        other = fc ^ 1
        swapped[other * lines:(other + 1) * lines, :] = rounded if fc % 2 == 0 else -rounded

    def screened(lay, load):
        sine, cosine = screen_of(lay)
        for f in range(2):
            re = load(2 * f)
            im = load(2 * f + 1)
            put(2 * f, re * cosine - im * sine)
            put(2 * f + 1, re * sine + im * cosine)

    block = 256

    def across(lay, step):
        per = block // lines

        def body(i, _):
            b = lax.rem(me // per + 1 + i, length // block)
            at = pl.ds(pl.multiple_of(b * block, block), block)
            dims = (((1,), (1,)), ((), ()))
            total = lax.dot_general(
                gmat[lay, 0, at, :], slab[...], dims, preferred_element_type=F32
            ) + lax.dot_general(
                gmat[lay, 1, at, :], swapped[...], dims, preferred_element_type=F32
            )
            sendbuf[step, pl.ds(b * per, per)] = total.reshape(per, lines, wide).astype(BF16)

            def one(j, _):
                peer = b * per + lax.rem(me + j, per)

                @pl.when(peer != me)
                def _():
                    remote(
                        sendbuf.at[step, peer], recvbuf.at[step, me], xsend.at[step],
                        xrecv.at[step], lax.rem(peer, layers), peer // layers,
                    ).start()
                return 0

            lax.fori_loop(0, per, one, 0)
            return 0

        lax.fori_loop(0, length // block, body, 0)

        recvbuf[step, me] = sendbuf[step, me]

    def arrived(step):
        most = recvbuf.at[step, pl.ds(0, count - 1)]
        remote(most, most, xsend.at[step], xrecv.at[step], sec, strip).wait_recv()
        if wide == 128:
            lane = lax.broadcasted_iota(jnp.int32, (lines, wide), 1) // lines
            for g in range(count // 4):
                pieces = [recvbuf[step, 4 * g + q].astype(F32) for q in range(4)]
                for fc in range(4):
                    out = None
                    for q in range(4):
                        shift = ((q - fc) * lines) % wide
                        moved = pltpu.roll(pieces[q], shift, axis=1) if shift else pieces[q]
                        out = moved if out is None else jnp.where(lane == q, moved, out)
                    rounded = out.astype(BF16)
                    at = slice(g * wide, (g + 1) * wide)
                    slab[fc * lines:(fc + 1) * lines, at] = rounded
                    other = fc ^ 1
                    swapped[other * lines:(other + 1) * lines, at] = (
                        rounded if fc % 2 == 0 else -rounded
                    )
        else:
            for fc in range(4):
                put(fc, jnp.concatenate(
                    [
                        recvbuf[step, d].astype(F32)[:, fc * lines:(fc + 1) * lines]
                        for d in range(count)
                    ],
                    axis=1,
                ))

    def along(lay):
        def body(b, _):
            at = pl.ds(pl.multiple_of(b * block, block), block)
            mid[:, at] = jnp.dot(
                slab[...], gmat[lay, 0, :, at], preferred_element_type=F32
            ) + jnp.dot(swapped[...], gmat[lay, 1, :, at], preferred_element_type=F32)
            return 0

        lax.fori_loop(0, length // block, body, 0)

    build(0)
    screened(0, lambda fc: launch_ref[fc, sec].astype(F32))
    across(0, 0)
    for lay in range(1, layers):
        build(lay)
    for lay in range(1, layers):
        arrived(lay - 1)
        along(lay - 1)
        screened(lay, lambda fc: mid[fc * lines:(fc + 1) * lines, :])
        across(lay, lay)
    arrived(layers - 1)
    along(layers - 1)
    for fc in range(4):
        out_ref[sec, fc] = mid[fc * lines:(fc + 1) * lines, :].astype(BF16)
    for k in range(1, layers):
        a = lax.rem(sec + k, layers)
        remote(out_ref.at[sec], out_ref.at[sec], osend, orecv, a, strip).start()
    most = out_ref.at[pl.ds(0, layers - 1)]
    remote(most, most, osend, orecv, sec, strip).wait()
    for k in range(1, layers):
        remote(g_ref, gall.at[sec], gsend, grecv.at[sec], sec, strip).wait_send()
    for lay in range(layers):
        @pl.when(sec == lay)
        def _(lay=lay):
            if lay % 2 == 0:
                some = rows_of[lay // 2][0].at[pl.ds(0, layers - 1)]
            else:
                some = cols_of[lay // 2][0].at[pl.ds(0, count - 1)]
            remote(some, some, ssend, srecv.at[lay], sec, strip).wait_send()
    for step in range(layers):
        most = sendbuf.at[step, pl.ds(0, count - 1)]
        remote(most, most, xsend.at[step], xrecv.at[step], sec, strip).wait_send()


def propagate(launch, screens, line, layers, strips):
    rows, length = launch.shape[2:]
    lines = rows // layers
    count = layers * strips
    vmem = pl.BlockSpec(memory_space=pltpu.VMEM)
    dma = pltpu.SemaphoreType.DMA
    screen = screens[0]
    return pl.pallas_call(
        functools.partial(propagate_kernel, layers, strips),
        out_shape=jax.ShapeDtypeStruct((layers, 4, lines, length), BF16),
        in_specs=[vmem] * 4,
        out_specs=vmem,
        scratch_shapes=[
            pltpu.VMEM((layers, 8, length), F32),
            pltpu.VMEM((layers, 2, length, length), BF16),
            pltpu.VMEM((lines, length), BF16),
            pltpu.VMEM((strips, lines, rows), BF16),
            pltpu.VMEM((layers, lines, length), BF16),
            pltpu.VMEM((count, lines, rows), BF16),
            pltpu.VMEM((layers // 2 - 1, lines, length), F32),
            pltpu.VMEM((layers // 2 - 1, strips, lines, rows), F32),
            pltpu.VMEM((layers, count, lines, 4 * lines), BF16),
            pltpu.VMEM((layers, count, lines, 4 * lines), BF16),
            pltpu.VMEM((4 * lines, length), BF16),
            pltpu.VMEM((4 * lines, length), BF16),
            pltpu.VMEM((4 * lines, length), F32),
            dma, dma((layers,)), dma, dma((layers,)), dma((layers,)), dma((layers,)), dma, dma,
        ],
        compiler_params=pltpu.CompilerParams(
            collective_id=0, has_side_effects=True, vmem_limit_bytes=56 << 20
        ),
        name="propagate",
    )(
        launch.reshape(4, layers, lines, length),
        screen.reshape(layers, lines, length),
        screen.T.reshape(count, lines, rows),
        line,
    )


def gather_kernel(side, picks_ref, pupil_ref, out_ref):
    for o in range(out_ref.shape[0]):
        pick = picks_ref[o]
        top = pl.multiple_of(pick // side * SUB, SUB)
        left = pick % side * SUB
        tile = pl.multiple_of(left // 128 * 128, 128)
        shift = (128 - left % 128) % 128
        for part in range(4):
            rows = pupil_ref[part, pl.ds(top, SUB), pl.ds(tile, 128)].astype(F32)
            out_ref[o, part] = pltpu.roll(rows, shift, axis=1)[:, :SUB].astype(BF16)


def gather_blocks(pupil, picks):
    vmem = pl.BlockSpec(memory_space=pltpu.VMEM)
    return pl.pallas_call(
        functools.partial(gather_kernel, pupil.shape[-1] // SUB),
        out_shape=jax.ShapeDtypeStruct((picks.shape[0], 4, SUB, SUB), BF16),
        in_specs=[pl.BlockSpec(memory_space=pltpu.SMEM), vmem],
        out_specs=vmem,
        name="gather",
    )(picks, pupil)


def swap_kernel(strips, in_ref, out_ref, send, recv):
    sec = lax.axis_index("layer")
    strip = lax.axis_index("strip")
    barrier = pltpu.get_barrier_semaphore()
    for k in range(1, strips):
        pl.semaphore_signal(
            barrier, inc=1, device_id=(sec, lax.rem(strip + k, strips)), device_id_type=MESH
        )
    pl.semaphore_wait(barrier, strips - 1)
    for k in range(1, strips):
        peer = lax.rem(strip + k, strips)
        pltpu.make_async_remote_copy(
            src_ref=in_ref.at[peer], dst_ref=out_ref.at[strip], send_sem=send, recv_sem=recv,
            device_id=(sec, peer), device_id_type=MESH,
        ).start()
    out_ref[strip] = in_ref[strip]
    most = out_ref.at[pl.ds(0, strips - 1)]
    pltpu.make_async_remote_copy(
        src_ref=most, dst_ref=most, send_sem=send, recv_sem=recv,
        device_id=(sec, strip), device_id_type=MESH,
    ).wait()


def swap_strips(result, strips):
    fields, channels = result.shape[1:]
    vmem = pl.BlockSpec(memory_space=pltpu.VMEM)
    dma = pltpu.SemaphoreType.DMA
    out = pl.pallas_call(
        functools.partial(swap_kernel, strips),
        out_shape=jax.ShapeDtypeStruct((strips, 8, 128), F32),
        in_specs=[vmem],
        out_specs=vmem,
        scratch_shapes=[dma, dma],
        compiler_params=pltpu.CompilerParams(collective_id=1, has_side_effects=True),
        name="swap",
    )(jnp.pad(result, ((0, 0), (0, 8 - fields), (0, 128 - channels))))
    return out[:, :fields, :channels]


QUARTER = 256
TILE = 128
PIECE = 16


def spot_rows(subsize):
    table = np.asarray(spot_table(subsize))
    split = table.reshape(2, subsize, subsize // 4, 2, 2, table.shape[1])
    return split.transpose(2, 3, 0, 4, 1, 5).reshape(table.shape)


def spread(x):
    (r0, i0), (r1, i1), (r2, i2), (r3, i3) = x
    er, ei, fr, fi = r0 + r2, i0 + i2, r1 + r3, i1 + i3
    gr, gi, dr, di = r0 - r2, i0 - i2, r1 - r3, i1 - i3
    return [(er + fr, ei + fi), (gr - di, gi + dr), (er - fr, ei - fi), (gr + di, gi - dr)]


def collect(y):
    (r0, i0), (r1, i1), (r2, i2), (r3, i3) = y
    er, ei, fr, fi = r0 + r2, i0 + i2, r1 + r3, i1 + i3
    gr, gi, dr, di = r0 - r2, i0 - i2, r1 - r3, i1 - i3
    return [(er + fr, ei + fi), (gr + di, gi - dr), (er - fr, ei - fi), (gr - di, gi + dr)]


def fused_kernel(
    table_ref, counts_ref, distance_ref, templates_far, launch_ref, screen_ref, cosine_ref, spot_ref, out_ref, corr_ref,
    templates_ref, field, screen, cosine, spot, infos, lines_ref, gmat, stage, staget, hops, screen0, columns, screen2,
    sincos_ref, slab, swapped, ybuf, send1, recv1, send2, recv2, send3, recv3, send4, recv4,
    mine, select, flat, results, answers,
    lsem, ready, isend, irecv, ssend, srecv, fsend, frecv, xsend, xrecv, osend, orecv, csend, crecv,
):
    layers, strips, count = 4, 8, 32
    group = count // 2
    sec = lax.axis_index("layer")
    strip = lax.axis_index("strip")
    me = strip * layers + sec
    half = me // group
    place = lax.rem(me, group)

    screen1, screen3 = columns.at[pl.ds(0, strips)], columns.at[pl.ds(strips, strips)]

    copies = [
        pltpu.make_async_copy(screen_ref, screen, lsem.at[0]),
        pltpu.make_async_copy(launch_ref.at[:, sec], field, lsem.at[1]),
        pltpu.make_async_copy(cosine_ref, cosine, lsem.at[2]),
        pltpu.make_async_copy(spot_ref, spot, lsem.at[3]),
        pltpu.make_async_copy(templates_far, templates_ref, lsem.at[4]),
    ]
    for copy in copies:
        copy.start()

    barrier = pltpu.get_barrier_semaphore()
    for k in range(1, layers):
        pl.semaphore_signal(
            barrier, inc=1, device_id=(lax.rem(sec + k, layers), strip), device_id_type=MESH
        )
    for k in range(1, strips):
        pl.semaphore_signal(
            barrier, inc=1, device_id=(sec, lax.rem(strip + k, strips)), device_id_type=MESH
        )

    def remote(src, dst, ssem, rsem, dev):
        return pltpu.make_async_remote_copy(
            src_ref=src, dst_ref=dst, send_sem=ssem, recv_sem=rsem,
            device_id=(lax.rem(dev, layers), dev // layers), device_id_type=MESH,
        )

    results[...] = jnp.zeros_like(results)
    row8 = lax.broadcasted_iota(jnp.int32, (8, TILE), 0)
    table = jnp.zeros((8, TILE), jnp.int32)
    live = jnp.zeros((8, TILE), jnp.int32)
    for o in range(8):
        table = jnp.where(row8 == o, jnp.full((8, TILE), table_ref[o], jnp.int32), table)
        live = jnp.where(row8 == o, jnp.full((8, TILE), counts_ref[o], jnp.int32), live)
    infos[sec, 0:8, :] = jnp.where(live > sec, table, -4096).astype(F32)
    infos[sec, 8:16, :] = jnp.full((8, TILE), distance_ref[0], F32)
    copies[0].wait()

    @pl.when(lax.rem(sec, 2) == 0)
    def _():
        stage[...] = screen[...].astype(BF16)

    @pl.when(lax.rem(sec, 2) == 1)
    def _():
        staget[...] = screen[...].T.astype(BF16).reshape(4, 4, 64, TILE)

    pl.semaphore_wait(barrier, layers + strips - 2)

    twin = group * (1 - half) + place
    near = place // 8 == half
    mine2 = (sec == 2) & (place // 2 == strip)

    def share(lay):
        @pl.when(sec == lay)
        def _():
            if lay != 2:
                for k in range(1, layers):
                    a = (lay + k) % layers
                    remote(
                        staget.at[:, a], hops.at[lay // 2], ssend, srecv.at[lay], strip * layers + a
                    ).start()
                hops[lay // 2] = staget[:, lay]
                return
            for k in range(2):
                peer = group * half + lax.rem(2 * strip, group) + k
                src = stage.at[pl.ds(64 * k, 64)]

                @pl.when(peer != me)
                def _(peer=peer, src=src):
                    remote(src, screen2, ssend, srecv.at[2], peer).start()

                @pl.when(peer == me)
                def _(src=src):
                    screen2[...] = src[...]

    def pass_on(lay):
        if lay == 2:
            @pl.when(near & jnp.logical_not(mine2))
            def _():
                remote(screen2, screen2, ssend, srecv.at[2], me).wait_recv()

            @pl.when(near)
            def _():
                remote(screen2, screen2, fsend.at[2], frecv.at[2], twin).start()
            return
        ref = screen1 if lay == 1 else screen3

        hop = hops.at[lay // 2]

        @pl.when(sec != lay)
        def _():
            remote(hop, hop, ssend, srecv.at[lay], me).wait_recv()

        def one(k, _):
            other = lax.rem(strip + k, strips)
            remote(
                hop.at[lax.rem(other, 4)], ref.at[strip], fsend.at[lay], frecv.at[lay],
                other * layers + sec,
            ).start()
            return 0

        lax.fori_loop(1, strips, one, 0)
        ref[strip] = hop[lax.rem(strip, 4)]

    def passed(lay):
        if lay == 2:
            @pl.when(jnp.logical_not(near))
            def _():
                remote(screen2, screen2, fsend.at[2], frecv.at[2], me).wait_recv()
            return
        some = (screen1 if lay == 1 else screen3).at[pl.ds(0, strips - 1)]
        remote(some, some, fsend.at[lay], frecv.at[lay], me).wait_recv()

    for k in range(1, layers):
        peer = strip * layers + lax.rem(sec + k, layers)
        remote(infos.at[sec], infos.at[sec], isend, irecv, peer).start()

    @pl.when(sec == 0)
    def _():
        for k in range(1, layers):
            remote(
                stage.at[pl.ds(32 * k, 32)], screen0, ssend, srecv.at[0], strip * layers + k
            ).start()
        screen0[...] = stage[0:32, :]

    share(1)

    for k in range(1, layers):
        pl.semaphore_signal(
            ready, inc=1, device_id=(lax.rem(sec + k, layers), strip), device_id_type=MESH
        )

    most = infos.at[pl.ds(0, layers - 1)]
    remote(most, most, isend, irecv, me).wait_recv()
    copies[2].wait()

    dist = infos[3, 8:16, :]
    for lay in range(3):
        dist = jnp.where(row8 // 2 == lay, infos[lay, 8:16, :], dist)
    wide = jnp.concatenate([dist] * 4, axis=1)
    turn = 0.5 / float(1024 * 1024)

    def wave(d, squares):
        t = d * (squares * turn)
        t = t - jnp.round(t)
        sine, cosine_ = sincos(t * (-2.0 * math.pi))
        row = lax.broadcasted_iota(jnp.int32, d.shape, 0)
        return jnp.where(row % 2 == 0, cosine_, sine)

    k = lax.broadcasted_iota(jnp.int32, (8, 512), 1).astype(F32)
    weight = jnp.where(k == 0.0, 0.25, 0.5) / 1024.0
    folded = wave(wide, k * k) * weight
    high = folded.astype(BF16)
    low = (folded - high.astype(F32)).astype(BF16)
    parts = jnp.dot(
        jnp.concatenate([high.astype(F32), low.astype(F32)], axis=0).astype(BF16),
        cosine[...], preferred_element_type=F32,
    )
    last = wave(dist, jnp.full((8, TILE), 512.0 * 512.0, F32)) * (0.25 / 1024.0)
    lane8 = lax.broadcasted_iota(jnp.int32, (8, TILE), 1)
    last = jnp.where(lane8 % 2 == 0, last, -last)
    lines_ref[...] = parts[:8] + parts[8:] + jnp.concatenate([last] * 8, axis=1)

    def build(lay):
        quarters = []
        for q in range(4):
            at = slice(QUARTER * q, QUARTER * (q + 1))
            quarters.append((
                lines_ref[2 * lay:2 * lay + 1, at], lines_ref[2 * lay + 1:2 * lay + 2, at]
            ))
        for b, (re, im) in enumerate(spread(quarters)):
            turned = [(re, im), (-im, re), (-re, -im), (im, -re)][b]
            for part, (first, second) in enumerate([(turned[0], re), (turned[1], im)]):
                row = jnp.concatenate([first, second], axis=1)
                base = pltpu.roll(
                    jnp.broadcast_to(row, (TILE, 2 * QUARTER)), 0, axis=1, stride=1, stride_axis=0
                ).astype(BF16)
                gmat[lay, b, part, 0:TILE, :] = base[:, 2 * TILE:4 * TILE]
                gmat[lay, b, part, TILE:2 * TILE, :] = base[:, TILE:3 * TILE]

    def angles(lay):
        if lay == 0:
            @pl.when(sec != 0)
            def _():
                remote(screen0, screen0, ssend, srecv.at[0], me).wait_recv()

            for r in range(0, 32, PIECE):
                sine, cosine_ = sincos(screen0[r:r + PIECE, :].astype(F32))
                sincos_ref[0, r:r + PIECE, :] = sine
                sincos_ref[1, r:r + PIECE, :] = cosine_
            return
        passed(lay)
        if lay == 2:
            for r in range(0, 64, PIECE):
                sine, cosine_ = sincos(screen2[r:r + PIECE, :].astype(F32))
                sincos_ref[0, r:r + PIECE, :] = sine
                sincos_ref[1, r:r + PIECE, :] = cosine_
            return
        ref = screen1 if lay == 1 else screen3
        for s in range(strips):
            sine, cosine_ = sincos(ref[s].astype(F32))
            sincos_ref[0, :, TILE * s:TILE * (s + 1)] = sine
            sincos_ref[1, :, TILE * s:TILE * (s + 1)] = cosine_

    def put(b, re_at, im_at, c, re, im):
        lanes = slice(TILE * c, TILE * (c + 1))
        re = re.astype(BF16)
        im = im.astype(BF16)
        slab[b, re_at:re_at + PIECE, lanes] = re
        slab[b, im_at:im_at + PIECE, lanes] = im
        swapped[b, re_at:re_at + PIECE, lanes] = -im
        swapped[b, im_at:im_at + PIECE, lanes] = re

    def put_all(re_at, im_at, c, x):
        for b, (re, im) in enumerate(spread(x)):
            put(b, re_at, im_at, c, re, im)

    def pieces(split):
        if split:
            return [(r, 64 + r, r) for r in range(0, 64, PIECE)]
        return [(64 * f + r, 64 * f + 32 + r, r) for f in range(2) for r in range(0, 32, PIECE)]

    def screened(x, line, c):
        out = []
        for q, (re, im) in enumerate(x):
            lanes = slice(QUARTER * q + TILE * c, QUARTER * q + TILE * (c + 1))
            sine = sincos_ref[0, line:line + PIECE, lanes]
            cosine_ = sincos_ref[1, line:line + PIECE, lanes]
            out.append((re * cosine_ - im * sine, re * sine + im * cosine_))
        return out

    def finished(re_at, im_at, c):
        lanes = slice(TILE * c, TILE * (c + 1))
        return collect([
            (ybuf[b, re_at:re_at + PIECE, lanes], ybuf[b, im_at:im_at + PIECE, lanes])
            for b in range(4)
        ])

    def along(lay, first=0, number=TILE):
        at = slice(first, first + number)
        for b in range(4):
            ybuf[b, at, :] = jnp.dot(
                slab[b, at, :], gmat[lay, b, 0], preferred_element_type=F32
            ) + jnp.dot(swapped[b, at, :], gmat[lay, b, 1], preferred_element_type=F32)

    lane = lax.broadcasted_iota(jnp.int32, (32, TILE), 1)
    lower = lane < 64

    def across(lay, store, targets, send, recv, slot, step):
        dims = (((1,), (1,)), ((), ()))
        for chunk in range(2):
            at = slice(TILE * chunk, TILE * (chunk + 1))
            y = [
                lax.dot_general(
                    gmat[lay, (4 - b) % 4, 0, at, :], slab[b], dims, preferred_element_type=F32
                ) + lax.dot_general(
                    gmat[lay, (4 - b) % 4, 1, at, :], swapped[b], dims, preferred_element_type=F32
                )
                for b in range(4)
            ]
            for r in range(0, TILE, 32):
                y0, y1, y2, y3 = [v[r:r + 32, :] for v in y]
                even, odd, both, gap = y0 + y2, y0 - y2, y1 + y3, y1 - y3
                if step == 0:
                    turned = jnp.where(
                        lane % 64 < 32, -pltpu.roll(gap, TILE - 32, axis=1), pltpu.roll(gap, 32, axis=1)
                    )
                else:
                    moved = pltpu.roll(gap, 64, axis=1)
                    turned = jnp.where(lower, -moved, moved)
                for q, v in enumerate([even + both, odd - turned, even - both, odd + turned]):
                    store(q, chunk, r, v)

            def one(i, _, chunk=chunk):
                dev, index = targets(lax.rem(i + me, 16 if step in (0, 3) else 8), chunk)

                @pl.when(dev != me)
                def _():
                    src, dst = (send.at[0], recv.at[0]) if step == 3 else (send, recv)
                    remote(
                        src.at[index], dst.at[slot], xsend.at[step], xrecv.at[step], dev
                    ).start()
                return 0

            lax.fori_loop(0, 16 if step in (0, 3) else 8, one, 0)

        if step == 3:
            def late(i, _):
                dev = lax.rem(i + me, count)
                remote(
                    send.at[1, dev], recv.at[1, me], xsend.at[4], xrecv.at[4], dev
                ).start()
                return 0

            lax.fori_loop(1, count, late, 0)

    held = {}

    def store_first(q, chunk, r, v):
        p = 4 * q + 2 * chunk + r // 64
        if r % 64 == 0:
            held[q] = v
            return
        top, bottom = held[q], v
        send1[p] = jnp.where(lower, top, pltpu.roll(bottom, 64, axis=1)).astype(BF16)
        send1[group + p] = jnp.where(lower, pltpu.roll(top, 64, axis=1), bottom).astype(BF16)

    def targets_first(i, chunk):
        dev = group * (i // 8) + 4 * lax.rem(i // 2, 4) + 2 * chunk + lax.rem(i, 2)
        return dev, dev

    def store_middle(send):
        def store(q, chunk, r, v):
            send[4 * q + 2 * chunk + r // 64, r % 64:r % 64 + 32, :] = v.astype(BF16)
        return store

    def targets_middle(i, chunk):
        p = 4 * (i // 2) + 2 * chunk + lax.rem(i, 2)
        return group * half + p, p

    def store_last(q, chunk, r, v):
        for n in range(2):
            send4[n, 8 * q + 4 * chunk + r // 32] = v[16 * n:16 * (n + 1), :].astype(BF16)

    def targets_last(i, chunk):
        dev = 8 * (i // 4) + 4 * chunk + lax.rem(i, 4)
        return dev, dev

    def wait_arrival(recv, number, step):
        some = recv.at[pl.ds(0, number)]
        remote(some, some, xsend.at[step], xrecv.at[step], me).wait_recv()

    def arrive_first():
        recv1[me] = send1[me]
        wait_arrival(recv1, count - 1, 0)
        small = lax.broadcasted_iota(jnp.int32, (PIECE, TILE), 1) // 32
        for c in range(2):
            for r in range(0, 32, PIECE):
                tiles = []
                for q in range(4):
                    g = 2 * q + c
                    got = [recv1[4 * g + s, r:r + PIECE, :].astype(F32) for s in range(4)]
                    outs = []
                    for fc in range(4):
                        out = None
                        for s in range(4):
                            shift = ((s - fc) * 32) % TILE
                            moved = pltpu.roll(got[s], shift, axis=1) if shift else got[s]
                            out = moved if out is None else jnp.where(small == s, moved, out)
                        outs.append(out)
                    tiles.append(outs)
                for e in range(2):
                    at = 32 * e + r
                    put_all(at, 64 + at, c, [(t[2 * e], t[2 * e + 1]) for t in tiles])

    low16 = lax.broadcasted_iota(jnp.int32, (PIECE, TILE), 1) < 64

    def joined(recv, base, g, r):
        one = recv[base + 2 * g, r:r + PIECE, :].astype(F32)
        two = recv[base + 2 * g + 1, r:r + PIECE, :].astype(F32)
        return (
            jnp.where(low16, one, pltpu.roll(two, 64, axis=1)),
            jnp.where(low16, pltpu.roll(one, 64, axis=1), two),
        )

    def arrive_middle(send, recv, step):
        recv[place] = send[place]
        wait_arrival(recv, group - 1, step)
        for c in range(2):
            for r in range(0, 64, PIECE):
                put_all(r, 64 + r, c, [joined(recv, 0, 2 * q + c, r) for q in range(4)])

    def arrive_last(n):
        recv, send = recv4.at[n], send4.at[n]
        recv[me] = send[me]
        wait_arrival(recv, count - 1, 3 + n)
        for c in range(2):
            for f in range(2):
                at = 64 * n + 32 * f
                put_all(
                    at, at + 16, c, [joined(recv, group * f, 2 * q + c, 0) for q in range(4)]
                )

    def rescreen():
        for c in range(2):
            for re_at, im_at, line in pieces(True):
                put_all(re_at, im_at, c, screened(finished(re_at, im_at, c), line, c))

    build(0)
    copies[1].wait()
    pass_on(1)
    angles(0)
    for c in range(2):
        for n, (re_at, im_at, line) in enumerate(pieces(False)):
            f = n // 2
            x = []
            for q in range(4):
                lanes = slice(QUARTER * q + TILE * c, QUARTER * q + TILE * (c + 1))
                x.append((
                    field[2 * f, line:line + PIECE, lanes].astype(F32),
                    field[2 * f + 1, line:line + PIECE, lanes].astype(F32),
                ))
            put_all(re_at, im_at, c, screened(x, line, c))
    pl.semaphore_wait(ready, layers - 1)
    across(0, store_first, targets_first, send1, recv1, me, 0)

    share(2)
    share(3)
    for lay in range(1, layers):
        build(lay)
    pick = jnp.concatenate([infos[a, 0:8, :] for a in range(layers)], axis=0)
    block_row = jnp.floor(pick * (1.0 / 64.0))
    left = (pick - 64.0 * block_row) * 16.0
    low_row = block_row - (2 * sec).astype(F32)
    left = jnp.where((low_row == 0.0) | (low_row == 1.0), left, -4096.0)
    lane_f = lane.astype(F32)
    for k in range(SUB):
        for t in range(8):
            select[32 * k:32 * (k + 1), TILE * t:TILE * (t + 1)] = jnp.where(
                lane_f + float(TILE * t - k) == left, 1.0, 0.0
            ).astype(BF16)

    angles(1)
    arrive_first()
    along(0)
    rescreen()
    across(1, store_middle(send2), targets_middle, send2, recv2, place, 1)
    pass_on(2)
    pass_on(3)
    angles(2)
    arrive_middle(send2, recv2, 1)
    along(1)
    rescreen()
    across(2, store_middle(send3), targets_middle, send3, recv3, place, 2)
    angles(3)
    arrive_middle(send3, recv3, 2)
    along(2)
    rescreen()
    across(3, store_last, targets_last, send4, recv4, me, 3)
    beside = strip * layers + sec + 1 - 2 * lax.rem(sec, 2)
    above = strip * layers + lax.rem(sec + 2, layers)

    def rows_of(n, owner):
        return pl.ds(pl.multiple_of(32 * owner + 16 * n, 16), 16)

    def publish(n):
        own = rows_of(n, sec)
        for fc in range(4):
            f, part = fc // 2, fc % 2
            out_ref[fc, own, :] = mine[64 * f + 32 * part + 16 * n:64 * f + 32 * part + 16 * n + 16, :]
        for k in range(2):
            part = out_ref.at[pl.ds(2 * k, 2), own]
            remote(part, part, osend.at[n, 0, k], orecv.at[n, 0, k], beside).start()
            part = out_ref.at[pl.ds(2 - 2 * k, 2), own]
            remote(part, part, osend.at[n, 1, k], orecv.at[n, 1, k], above).start()

    def relay(n):
        part = out_ref.at[pl.ds(0, 2), rows_of(n, sec)]
        remote(part, part, osend.at[n, 0, 0], orecv.at[n, 0, 0], me).wait_recv()
        given = out_ref.at[pl.ds(0, 2), rows_of(n, sec + 1 - 2 * lax.rem(sec, 2))]
        remote(given, given, osend.at[n, 2, 0], orecv.at[n, 2, 0], above).start()
        remote(part, part, osend.at[n, 1, 0], orecv.at[n, 1, 0], me).wait_recv()
        given = out_ref.at[pl.ds(2, 2), rows_of(n, lax.rem(sec + 2, layers))]
        remote(given, given, osend.at[n, 2, 1], orecv.at[n, 2, 1], beside).start()

    for n in range(2):
        arrive_last(n)
        along(3, 64 * n, 64)
        for c in range(2):
            for f in range(2):
                at = 64 * n + 32 * f
                for q, (re, im) in enumerate(finished(at, at + 16, c)):
                    lanes = slice(QUARTER * q + TILE * c, QUARTER * q + TILE * (c + 1))
                    to = 64 * f + 16 * n
                    mine[to:to + PIECE, lanes] = re.astype(BF16)
                    mine[to + 32:to + 32 + PIECE, lanes] = im.astype(BF16)
        publish(n)
    relay(0)

    copies[3].wait()
    copies[4].wait()
    lane_row = lax.rem(lane // SUB, 2)
    match = lane_row.astype(F32) == low_row
    dims = (((1,), (1,)), ((), ()))
    taken = lax.dot_general(select[...], mine[...], dims, preferred_element_type=F32)
    folds = []
    for k in range(0, SUB, 2):
        x = jnp.where(match, taken[32 * k:32 * (k + 1), :], 0.0)
        x2 = jnp.where(match, taken[32 * (k + 1):32 * (k + 2), :], 0.0)
        x = x + pltpu.roll(x, TILE - SUB, axis=1)
        x2 = x2 + pltpu.roll(x2, SUB, axis=1)
        folds.append(jnp.where(lane_row == 0, x, x2))
    for m in range(4):
        c0, c1 = folds[2 * m], folds[2 * m + 1]
        lanes = slice(TILE * m, TILE * (m + 1))
        flat[0:32, lanes] = jnp.where(lower, c0, pltpu.roll(c1, 64, axis=1)).astype(BF16)
        flat[32:64, lanes] = jnp.where(lower, pltpu.roll(c0, 64, axis=1), c1).astype(BF16)
    total = jnp.zeros((64, 16), F32)
    for n in range(4):
        at = slice(256 * n, 256 * (n + 1))
        past = slice(1024 + 256 * n, 1024 + 256 * (n + 1))
        re = jnp.dot(flat[...], spot[:, at], preferred_element_type=F32)
        im = jnp.dot(flat[...], spot[:, past], preferred_element_type=F32)
        total = total + lax.dot_general(
            (re * re + im * im).astype(BF16), templates_ref[:, at], dims, preferred_element_type=F32
        )
    for f in range(2):
        results[:, f, 0:16] = total[32 * f:32 * (f + 1), :]

    def answer(i, _):
        dev = lax.rem(me + i, count)
        index = 8 * lax.rem(dev, layers) + dev // layers
        remote(results.at[index], answers.at[me], csend, crecv, dev).start()
        return 0

    lax.fori_loop(1, count, answer, 0)
    answers[me] = results[8 * sec + strip]

    relay(1)
    for n in range(2):
        part = out_ref.at[pl.ds(0, 2), rows_of(n, sec)]
        for k in range(2):
            for way in range(3):
                copy = remote(part, part, osend.at[n, way, k], orecv.at[n, way, k], me)
                copy.wait_send()
                if way == 2 or k == 1:
                    copy.wait_recv()
    some = answers.at[pl.ds(0, count - 1)]
    remote(some, some, csend, crecv, me).wait()
    for s in range(strips):
        block = answers[layers * s]
        for a in range(1, layers):
            block = block + answers[layers * s + a]
        corr_ref[s] = block[0:2, 0:16]

    some = infos.at[pl.ds(0, layers - 1)]
    remote(some, some, isend, irecv, me).wait_send()

    @pl.when(sec == 0)
    def _():
        some = stage.at[pl.ds(0, 96)]
        remote(some, some, ssend, srecv.at[0], me).wait_send()

    @pl.when(lax.rem(sec, 2) == 1)
    def _():
        some = columns.at[pl.ds(0, 12)]
        remote(some, some, ssend, srecv.at[1], me).wait_send()

    @pl.when((sec == 2) & mine2)
    def _():
        remote(screen2, screen2, ssend, srecv.at[2], me).wait_send()

    @pl.when((sec == 2) & jnp.logical_not(mine2))
    def _():
        remote(stage, stage, ssend, srecv.at[2], me).wait_send()

    @pl.when(near)
    def _():
        remote(screen2, screen2, fsend.at[2], frecv.at[2], me).wait_send()

    for lay, ref in ((1, screen1), (3, screen3)):
        some = ref.at[pl.ds(0, strips - 1)]
        remote(some, some, fsend.at[lay], frecv.at[lay], me).wait_send()

    for step, (send, number) in enumerate(
        [(send1, count), (send2, group), (send3, group), (send4.at[0], count), (send4.at[1], count)]
    ):
        some = send.at[pl.ds(0, number - 1)]
        remote(some, some, xsend.at[step], xrecv.at[step], me).wait_send()


def fused(launch, screens, distance, templates, send_table, send_counts):
    rows, length = launch.shape[2:]
    vmem = pl.BlockSpec(memory_space=pltpu.VMEM)
    smem = pl.BlockSpec(memory_space=pltpu.SMEM)
    far = pl.BlockSpec(memory_space=pltpu.HBM)
    dma = pltpu.SemaphoreType.DMA

    def blocks(number, height):
        return pltpu.VMEM((number, height, TILE), BF16)

    return pl.pallas_call(
        fused_kernel,
        out_shape=(
            jax.ShapeDtypeStruct((4, rows, length), BF16),
            jax.ShapeDtypeStruct((8, 2, 16), F32),
        ),
        in_specs=[smem, smem, smem, far, far, far, far, far],
        out_specs=(vmem, vmem),
        scratch_shapes=[
            pltpu.VMEM(templates.shape[::-1], BF16),
            pltpu.VMEM((4, 32, length), BF16),
            pltpu.VMEM((rows, length), F32),
            pltpu.VMEM((length // 2, length), BF16),
            pltpu.VMEM((512, 2048), BF16),
            pltpu.VMEM((4, 16, TILE), F32),
            pltpu.VMEM((8, length), F32),
            pltpu.VMEM((4, 4, 2, QUARTER, QUARTER), BF16),
            pltpu.VMEM((rows, length), BF16),
            pltpu.VMEM((4, 4, 64, TILE), BF16),
            pltpu.VMEM((2, 4, 64, TILE), BF16),
            pltpu.VMEM((32, length), BF16),
            pltpu.VMEM((16, 64, TILE), BF16),
            pltpu.VMEM((64, length), BF16),
            pltpu.VMEM((2, 64, length), F32),
            pltpu.VMEM((4, TILE, QUARTER), BF16),
            pltpu.VMEM((4, TILE, QUARTER), BF16),
            pltpu.VMEM((4, TILE, QUARTER), F32),
            blocks(32, 32), blocks(32, 32),
            blocks(16, 64), blocks(16, 64),
            blocks(16, 64), blocks(16, 64),
            pltpu.VMEM((2, 32, 16, TILE), BF16), pltpu.VMEM((2, 32, 16, TILE), BF16),
            pltpu.VMEM((TILE, length), BF16),
            pltpu.VMEM((512, length), BF16),
            pltpu.VMEM((64, 512), BF16),
            pltpu.VMEM((32, 2, TILE), F32),
            pltpu.VMEM((32, 2, TILE), F32),
            dma((5,)), pltpu.SemaphoreType.REGULAR, dma, dma, dma, dma((4,)), dma((4,)), dma((4,)),
            dma((5,)), dma((5,)), dma((2, 3, 2)), dma((2, 3, 2)), dma, dma,
        ],
        compiler_params=pltpu.CompilerParams(
            collective_id=2, has_side_effects=True, vmem_limit_bytes=60 << 20
        ),
        name="fused",
    )(
        send_table.reshape(8), send_counts.reshape(8), distance, templates.T, launch.reshape(4, 4, 32, length), screens[0],
        jnp.asarray(cosine_half_table(length)), jnp.asarray(spot_rows(SUB)),
    )


def finish_kernel(pupil_ref, found_ref, pupil_out, found_out, pupil, found, gets, puts):
    pairs = [(found_ref, found, found_out)]
    pairs += [(pupil_ref.at[n], pupil.at[n], pupil_out.at[n]) for n in range(4)]
    reads = [pltpu.make_async_copy(s, m, gets.at[n]) for n, (s, m, _) in enumerate(pairs)]
    writes = [pltpu.make_async_copy(m, d, puts.at[n]) for n, (_, m, d) in enumerate(pairs)]
    for copy in reads:
        copy.start()
    for read, write in zip(reads, writes):
        read.wait()
        write.start()
    for write in writes:
        write.wait()


def finish(pupil, found):
    far = pl.BlockSpec(memory_space=pltpu.HBM)
    dma = pltpu.SemaphoreType.DMA
    return pl.pallas_call(
        finish_kernel,
        out_shape=tuple(jax.ShapeDtypeStruct(x.shape, x.dtype) for x in (pupil, found)),
        in_specs=[far, far],
        out_specs=(far, far),
        scratch_shapes=[
            pltpu.VMEM(pupil.shape, pupil.dtype), pltpu.VMEM(found.shape, found.dtype),
            dma((5,)), dma((5,)),
        ],
        compiler_params=pltpu.CompilerParams(vmem_limit_bytes=60 << 20),
        name="finish",
    )(pupil, found)


def per_device_fused(launch, screens, distance, templates, send_table, send_counts):
    rows, length = launch.shape[2:]
    pupil, found = finish(
        *fused(launch, screens, distance, templates, send_table, send_counts)
    )
    return pupil.reshape(2, 2, rows, length), found[None, :, None]


def per_device(launch, screens, distance, templates, send_table, send_counts):
    layers = lax.axis_size("layer")
    strips = lax.axis_size("strip")
    sec = lax.axis_index("layer")
    fields = launch.shape[0]
    rows, length = launch.shape[2:]
    line = kernel_line(distance[0], length)
    done = propagate(launch, screens, line, layers, strips)
    pupil = done.transpose(1, 0, 2, 3).reshape(fields, 2, rows, length)
    side = length // SUB
    blocks = gather_blocks(pupil.reshape(2 * fields, rows, length), send_table.reshape(strips))
    flat = blocks.reshape(strips * fields, 2 * SUB * SUB)
    table = jnp.asarray(spot_table(SUB))
    pixels = templates.shape[0]
    spot = jnp.dot(flat, table, preferred_element_type=F32)
    intensity = (spot[:, :pixels] ** 2 + spot[:, pixels:] ** 2).astype(BF16)
    result = jnp.dot(intensity, templates, preferred_element_type=F32)
    result = result.reshape(strips, fields, templates.shape[1])
    live = sec < send_counts[0]
    result = jnp.where(live[:, None, None], result, 0.0)
    received = swap_strips(result, strips)
    return (pupil, received[None, :, None])


def solution(mesh):
    placed = (
        P(None, None, "strip", None),
        P("layer", "strip", None),
        P("layer"),
        P(),
        P("strip", None, "layer"),
        P("strip", None),
    )
    small = mesh.shape["layer"] == 4 and mesh.shape["strip"] == 8
    return jax.shard_map(
        per_device_fused if small else per_device,
        mesh=mesh,
        in_specs=placed,
        out_specs=(P(None, None, "strip", None), P("strip", None, "layer", None, None)),
        check_vma=False,
    )
```

```python
import functools
import math

import jax
import jax.numpy as jnp
import numpy as np
from jax import lax
from jax.experimental import pallas as pl
from jax.experimental.pallas import tpu as pltpu
from jax.sharding import PartitionSpec as P

SUB = 16
F32 = jnp.float32
BF16 = jnp.bfloat16
MESH = pl.DeviceIdType.MESH


def cosine_half_table(length):
    k = np.arange(length // 2, dtype=np.int64)
    n = np.arange(length, dtype=np.int64)
    p = (k[:, None] * n[None, :]) % length
    p = np.minimum(p, length - p)
    return np.cos(2.0 * np.pi * p / length).astype(np.float32).astype(BF16)


def spot_table(subsize):
    spotsize = 2 * subsize
    outer = np.arange(spotsize)
    inner = np.arange(subsize)
    angles = (inner[:, None] * outer[None, :] % spotsize) * (2.0 * np.pi / spotsize)
    wave = (np.cos(angles) - 1j * np.sin(angles)) / math.sqrt(subsize)
    kron = wave[:, None, :, None] * wave[None, :, None, :]
    kron = kron.reshape(subsize * subsize, spotsize * spotsize)
    upper = np.concatenate([kron.real, kron.imag], axis=1)
    lower = np.concatenate([-kron.imag, kron.real], axis=1)
    return np.concatenate([upper, lower], axis=0).astype(np.float32).astype(BF16)


def kernel_line(distance_value, length):
    half = length // 2
    counter = jnp.arange(half + 1, dtype=jnp.int32).astype(F32)
    phases = -distance_value * math.pi * counter * counter / float(length * length)
    h = jnp.stack([jnp.cos(phases), jnp.sin(phases)])
    weight = jnp.where(counter == 0.0, 1.0, 2.0) / length
    folded = (h * weight)[:, :half]
    high = folded.astype(BF16)
    low = (folded - high.astype(F32)).astype(BF16)
    table = jnp.asarray(cosine_half_table(length))
    parts = jnp.dot(jnp.concatenate([high, low]), table, preferred_element_type=F32)
    sign = (1 - 2 * (jnp.arange(length, dtype=jnp.int32) % 2)).astype(F32) / length
    line = parts[:2] + parts[2:] + h[:, half:] * sign
    return jnp.concatenate([line, jnp.zeros((6, length), F32)])


def sincos(x):
    y = 0.5 * x
    z = y * y
    s = -1.0 / 39916800.0
    for c in (1.0 / 362880.0, -1.0 / 5040.0, 1.0 / 120.0, -1.0 / 6.0, 1.0):
        s = s * z + c
    s = s * y
    c0 = 1.0 / 479001600.0
    for c in (-1.0 / 3628800.0, 1.0 / 40320.0, -1.0 / 720.0, 1.0 / 24.0, -0.5, 1.0):
        c0 = c0 * z + c
    return 2.0 * s * c0, 1.0 - 2.0 * s * s


def propagate_kernel(
    layers, strips, launch_ref, scr_ref, scrt_ref, g_ref, out_ref,
    gall, gmat, early_row, early_col, stage_row, stage_col, srow, scol, sendbuf, recvbuf, slab, swapped, mid,
    gsend, grecv, ssend, srecv, xsend, xrecv, osend, orecv,
):
    count = layers * strips
    length = launch_ref.shape[-1]
    lines = launch_ref.shape[-2]
    wide = 4 * lines
    sec = lax.axis_index("layer")
    strip = lax.axis_index("strip")
    me = strip * layers + sec

    barrier = pltpu.get_barrier_semaphore()

    def greet(k, _):
        peer = lax.rem(me + k, count)
        pl.semaphore_signal(
            barrier, inc=1, device_id=(lax.rem(peer, layers), peer // layers), device_id_type=MESH
        )
        return 0

    lax.fori_loop(1, count, greet, 0)
    pl.semaphore_wait(barrier, count - 1)

    def remote(src, dst, ssem, rsem, a, s):
        return pltpu.make_async_remote_copy(
            src_ref=src, dst_ref=dst, send_sem=ssem, recv_sem=rsem,
            device_id=(a, s), device_id_type=MESH,
        )

    for k in range(1, layers):
        a = lax.rem(sec + k, layers)
        remote(g_ref, gall.at[sec], gsend, grecv.at[sec], a, strip).start()
    def to_all(start_one):
        def one(k, _):
            peer = lax.rem(me + k, count)
            start_one(lax.rem(peer, layers), peer // layers)
            return 0

        lax.fori_loop(1, count, one, 0)

    rows_of = [(stage_row, early_row)] + [(scr_ref, srow.at[i]) for i in range(layers // 2 - 1)]
    cols_of = [(stage_col, early_col)] + [(scrt_ref, scol.at[i]) for i in range(layers // 2 - 1)]

    def share(lay):
        @pl.when(sec == lay)
        def _():
            if lay % 2 == 0:
                src, dst = rows_of[lay // 2]
                if lay < 2:
                    src[...] = scr_ref[...].astype(BF16)
                for k in range(1, layers):
                    a = lax.rem(sec + k, layers)
                    remote(src.at[a], dst, ssend, srecv.at[lay], a, strip).start()
                dst[...] = src[lay]
            else:
                src, dst = cols_of[lay // 2]
                if lay < 2:
                    src[...] = scrt_ref[...].astype(BF16)

                def one(a, s):
                    remote(
                        src.at[s * layers + a], dst.at[strip], ssend, srecv.at[lay], a, s
                    ).start()

                to_all(one)
                dst[strip] = src[me]

    for lay in range(layers):
        share(lay)
    gall[sec] = g_ref[...]

    def build(lay):
        @pl.when(sec != lay)
        def _():
            remote(g_ref, gall.at[lay], gsend, grecv.at[lay], sec, strip).wait_recv()

        band = 128
        for part in range(2):
            row = gall[lay, part:part + 1, :]
            base = pltpu.roll(
                jnp.broadcast_to(row, (band, length)), 0, axis=1, stride=1, stride_axis=0
            ).astype(BF16)
            for b in range(length // band):
                at = band * b
                if b:
                    gmat[lay, part, at:at + band, 0:at] = base[:, length - at:]
                gmat[lay, part, at:at + band, at:] = base[:, :length - at]

    def screen_of(lay):
        if lay % 2 == 0:
            src, dst = rows_of[lay // 2]

            @pl.when(sec != lay)
            def _():
                remote(src.at[0], dst, ssend, srecv.at[lay], sec, strip).wait_recv()
            return sincos(dst[...].astype(F32))

        dst = cols_of[lay // 2][1]

        @pl.when(sec != lay)
        def _():
            remote(dst, dst, ssend, srecv.at[lay], sec, strip).wait_recv()

        @pl.when(sec == lay)
        def _():
            most = dst.at[pl.ds(0, strips - 1)]
            remote(most, most, ssend, srecv.at[lay], sec, strip).wait_recv()

        return sincos(jnp.concatenate([dst[s].astype(F32) for s in range(strips)], axis=1))

    def put(fc, value):
        rounded = value.astype(BF16)
        slab[fc * lines:(fc + 1) * lines, :] = rounded
        other = fc ^ 1
        swapped[other * lines:(other + 1) * lines, :] = rounded if fc % 2 == 0 else -rounded

    def screened(lay, load):
        sine, cosine = screen_of(lay)
        for f in range(2):
            re = load(2 * f)
            im = load(2 * f + 1)
            put(2 * f, re * cosine - im * sine)
            put(2 * f + 1, re * sine + im * cosine)

    block = 256

    def across(lay, step):
        per = block // lines

        def body(i, _):
            b = lax.rem(me // per + 1 + i, length // block)
            at = pl.ds(pl.multiple_of(b * block, block), block)
            dims = (((1,), (1,)), ((), ()))
            total = lax.dot_general(
                gmat[lay, 0, at, :], slab[...], dims, preferred_element_type=F32
            ) + lax.dot_general(
                gmat[lay, 1, at, :], swapped[...], dims, preferred_element_type=F32
            )
            sendbuf[step, pl.ds(b * per, per)] = total.reshape(per, lines, wide).astype(BF16)

            def one(j, _):
                peer = b * per + lax.rem(me + j, per)

                @pl.when(peer != me)
                def _():
                    remote(
                        sendbuf.at[step, peer], recvbuf.at[step, me], xsend.at[step],
                        xrecv.at[step], lax.rem(peer, layers), peer // layers,
                    ).start()
                return 0

            lax.fori_loop(0, per, one, 0)
            return 0

        lax.fori_loop(0, length // block, body, 0)

        recvbuf[step, me] = sendbuf[step, me]

    def arrived(step):
        most = recvbuf.at[step, pl.ds(0, count - 1)]
        remote(most, most, xsend.at[step], xrecv.at[step], sec, strip).wait_recv()
        if wide == 128:
            lane = lax.broadcasted_iota(jnp.int32, (lines, wide), 1) // lines
            for g in range(count // 4):
                pieces = [recvbuf[step, 4 * g + q].astype(F32) for q in range(4)]
                for fc in range(4):
                    out = None
                    for q in range(4):
                        shift = ((q - fc) * lines) % wide
                        moved = pltpu.roll(pieces[q], shift, axis=1) if shift else pieces[q]
                        out = moved if out is None else jnp.where(lane == q, moved, out)
                    rounded = out.astype(BF16)
                    at = slice(g * wide, (g + 1) * wide)
                    slab[fc * lines:(fc + 1) * lines, at] = rounded
                    other = fc ^ 1
                    swapped[other * lines:(other + 1) * lines, at] = (
                        rounded if fc % 2 == 0 else -rounded
                    )
        else:
            for fc in range(4):
                put(fc, jnp.concatenate(
                    [
                        recvbuf[step, d].astype(F32)[:, fc * lines:(fc + 1) * lines]
                        for d in range(count)
                    ],
                    axis=1,
                ))

    def along(lay):
        def body(b, _):
            at = pl.ds(pl.multiple_of(b * block, block), block)
            mid[:, at] = jnp.dot(
                slab[...], gmat[lay, 0, :, at], preferred_element_type=F32
            ) + jnp.dot(swapped[...], gmat[lay, 1, :, at], preferred_element_type=F32)
            return 0

        lax.fori_loop(0, length // block, body, 0)

    build(0)
    screened(0, lambda fc: launch_ref[fc, sec].astype(F32))
    across(0, 0)
    for lay in range(1, layers):
        build(lay)
    for lay in range(1, layers):
        arrived(lay - 1)
        along(lay - 1)
        screened(lay, lambda fc: mid[fc * lines:(fc + 1) * lines, :])
        across(lay, lay)
    arrived(layers - 1)
    along(layers - 1)
    for fc in range(4):
        out_ref[sec, fc] = mid[fc * lines:(fc + 1) * lines, :].astype(BF16)
    for k in range(1, layers):
        a = lax.rem(sec + k, layers)
        remote(out_ref.at[sec], out_ref.at[sec], osend, orecv, a, strip).start()
    most = out_ref.at[pl.ds(0, layers - 1)]
    remote(most, most, osend, orecv, sec, strip).wait()
    for k in range(1, layers):
        remote(g_ref, gall.at[sec], gsend, grecv.at[sec], sec, strip).wait_send()
    for lay in range(layers):
        @pl.when(sec == lay)
        def _(lay=lay):
            if lay % 2 == 0:
                some = rows_of[lay // 2][0].at[pl.ds(0, layers - 1)]
            else:
                some = cols_of[lay // 2][0].at[pl.ds(0, count - 1)]
            remote(some, some, ssend, srecv.at[lay], sec, strip).wait_send()
    for step in range(layers):
        most = sendbuf.at[step, pl.ds(0, count - 1)]
        remote(most, most, xsend.at[step], xrecv.at[step], sec, strip).wait_send()


def propagate(launch, screens, line, layers, strips):
    rows, length = launch.shape[2:]
    lines = rows // layers
    count = layers * strips
    vmem = pl.BlockSpec(memory_space=pltpu.VMEM)
    dma = pltpu.SemaphoreType.DMA
    screen = screens[0]
    return pl.pallas_call(
        functools.partial(propagate_kernel, layers, strips),
        out_shape=jax.ShapeDtypeStruct((layers, 4, lines, length), BF16),
        in_specs=[vmem] * 4,
        out_specs=vmem,
        scratch_shapes=[
            pltpu.VMEM((layers, 8, length), F32),
            pltpu.VMEM((layers, 2, length, length), BF16),
            pltpu.VMEM((lines, length), BF16),
            pltpu.VMEM((strips, lines, rows), BF16),
            pltpu.VMEM((layers, lines, length), BF16),
            pltpu.VMEM((count, lines, rows), BF16),
            pltpu.VMEM((layers // 2 - 1, lines, length), F32),
            pltpu.VMEM((layers // 2 - 1, strips, lines, rows), F32),
            pltpu.VMEM((layers, count, lines, 4 * lines), BF16),
            pltpu.VMEM((layers, count, lines, 4 * lines), BF16),
            pltpu.VMEM((4 * lines, length), BF16),
            pltpu.VMEM((4 * lines, length), BF16),
            pltpu.VMEM((4 * lines, length), F32),
            dma, dma((layers,)), dma, dma((layers,)), dma((layers,)), dma((layers,)), dma, dma,
        ],
        compiler_params=pltpu.CompilerParams(
            collective_id=0, has_side_effects=True, vmem_limit_bytes=56 << 20
        ),
        name="propagate",
    )(
        launch.reshape(4, layers, lines, length),
        screen.reshape(layers, lines, length),
        screen.T.reshape(count, lines, rows),
        line,
    )


def gather_kernel(side, picks_ref, pupil_ref, out_ref):
    for o in range(out_ref.shape[0]):
        pick = picks_ref[o]
        top = pl.multiple_of(pick // side * SUB, SUB)
        left = pick % side * SUB
        tile = pl.multiple_of(left // 128 * 128, 128)
        shift = (128 - left % 128) % 128
        for part in range(4):
            rows = pupil_ref[part, pl.ds(top, SUB), pl.ds(tile, 128)].astype(F32)
            out_ref[o, part] = pltpu.roll(rows, shift, axis=1)[:, :SUB].astype(BF16)


def gather_blocks(pupil, picks):
    vmem = pl.BlockSpec(memory_space=pltpu.VMEM)
    return pl.pallas_call(
        functools.partial(gather_kernel, pupil.shape[-1] // SUB),
        out_shape=jax.ShapeDtypeStruct((picks.shape[0], 4, SUB, SUB), BF16),
        in_specs=[pl.BlockSpec(memory_space=pltpu.SMEM), vmem],
        out_specs=vmem,
        name="gather",
    )(picks, pupil)


def swap_kernel(strips, in_ref, out_ref, send, recv):
    sec = lax.axis_index("layer")
    strip = lax.axis_index("strip")
    barrier = pltpu.get_barrier_semaphore()
    for k in range(1, strips):
        pl.semaphore_signal(
            barrier, inc=1, device_id=(sec, lax.rem(strip + k, strips)), device_id_type=MESH
        )
    pl.semaphore_wait(barrier, strips - 1)
    for k in range(1, strips):
        peer = lax.rem(strip + k, strips)
        pltpu.make_async_remote_copy(
            src_ref=in_ref.at[peer], dst_ref=out_ref.at[strip], send_sem=send, recv_sem=recv,
            device_id=(sec, peer), device_id_type=MESH,
        ).start()
    out_ref[strip] = in_ref[strip]
    most = out_ref.at[pl.ds(0, strips - 1)]
    pltpu.make_async_remote_copy(
        src_ref=most, dst_ref=most, send_sem=send, recv_sem=recv,
        device_id=(sec, strip), device_id_type=MESH,
    ).wait()


def swap_strips(result, strips):
    fields, channels = result.shape[1:]
    vmem = pl.BlockSpec(memory_space=pltpu.VMEM)
    dma = pltpu.SemaphoreType.DMA
    out = pl.pallas_call(
        functools.partial(swap_kernel, strips),
        out_shape=jax.ShapeDtypeStruct((strips, 8, 128), F32),
        in_specs=[vmem],
        out_specs=vmem,
        scratch_shapes=[dma, dma],
        compiler_params=pltpu.CompilerParams(collective_id=1, has_side_effects=True),
        name="swap",
    )(jnp.pad(result, ((0, 0), (0, 8 - fields), (0, 128 - channels))))
    return out[:, :fields, :channels]


QUARTER = 256
TILE = 128
PIECE = 16


def spot_rows(subsize):
    table = np.asarray(spot_table(subsize))
    split = table.reshape(2, subsize, subsize // 4, 2, 2, table.shape[1])
    return split.transpose(2, 3, 0, 4, 1, 5).reshape(table.shape)


def spread(x):
    (r0, i0), (r1, i1), (r2, i2), (r3, i3) = x
    er, ei, fr, fi = r0 + r2, i0 + i2, r1 + r3, i1 + i3
    gr, gi, dr, di = r0 - r2, i0 - i2, r1 - r3, i1 - i3
    return [(er + fr, ei + fi), (gr - di, gi + dr), (er - fr, ei - fi), (gr + di, gi - dr)]


def collect(y):
    (r0, i0), (r1, i1), (r2, i2), (r3, i3) = y
    er, ei, fr, fi = r0 + r2, i0 + i2, r1 + r3, i1 + i3
    gr, gi, dr, di = r0 - r2, i0 - i2, r1 - r3, i1 - i3
    return [(er + fr, ei + fi), (gr + di, gi - dr), (er - fr, ei - fi), (gr - di, gi + dr)]


def fused_kernel(
    table_ref, counts_ref, distance_ref, templates_far, launch_ref, screen_ref, cosine_ref, spot_ref, out_ref, corr_ref,
    templates_ref, field, screen, cosine, spot, infos, lines_ref, gmat, stage, staget, hops, screen0, columns, screen2,
    sincos_ref, slab, swapped, ybuf, send1, recv1, send2, recv2, send3, recv3, send4, recv4,
    mine, pupil, select, flat, results, answers,
    lsem, ready, isend, irecv, ssend, srecv, fsend, frecv, xsend, xrecv, osend, orecv, csend, crecv, wsem,
):
    layers, strips, count = 4, 8, 32
    group = count // 2
    sec = lax.axis_index("layer")
    strip = lax.axis_index("strip")
    me = strip * layers + sec
    half = me // group
    place = lax.rem(me, group)

    screen1, screen3 = columns.at[pl.ds(0, strips)], columns.at[pl.ds(strips, strips)]

    copies = [
        pltpu.make_async_copy(screen_ref, screen, lsem.at[0]),
        pltpu.make_async_copy(launch_ref.at[:, sec], field, lsem.at[1]),
        pltpu.make_async_copy(cosine_ref, cosine, lsem.at[2]),
        pltpu.make_async_copy(spot_ref, spot, lsem.at[3]),
        pltpu.make_async_copy(templates_far, templates_ref, lsem.at[4]),
    ]
    for copy in copies:
        copy.start()

    barrier = pltpu.get_barrier_semaphore()
    for k in range(1, layers):
        pl.semaphore_signal(
            barrier, inc=1, device_id=(lax.rem(sec + k, layers), strip), device_id_type=MESH
        )
    for k in range(1, strips):
        pl.semaphore_signal(
            barrier, inc=1, device_id=(sec, lax.rem(strip + k, strips)), device_id_type=MESH
        )

    def remote(src, dst, ssem, rsem, dev):
        return pltpu.make_async_remote_copy(
            src_ref=src, dst_ref=dst, send_sem=ssem, recv_sem=rsem,
            device_id=(lax.rem(dev, layers), dev // layers), device_id_type=MESH,
        )

    results[...] = jnp.zeros_like(results)
    row8 = lax.broadcasted_iota(jnp.int32, (8, TILE), 0)
    table = jnp.zeros((8, TILE), jnp.int32)
    live = jnp.zeros((8, TILE), jnp.int32)
    for o in range(8):
        table = jnp.where(row8 == o, jnp.full((8, TILE), table_ref[o], jnp.int32), table)
        live = jnp.where(row8 == o, jnp.full((8, TILE), counts_ref[o], jnp.int32), live)
    infos[sec, 0:8, :] = jnp.where(live > sec, table, -4096).astype(F32)
    infos[sec, 8:16, :] = jnp.full((8, TILE), distance_ref[0], F32)
    copies[0].wait()

    @pl.when(lax.rem(sec, 2) == 0)
    def _():
        stage[...] = screen[...].astype(BF16)

    @pl.when(lax.rem(sec, 2) == 1)
    def _():
        staget[...] = screen[...].T.astype(BF16).reshape(4, 4, 64, TILE)

    pl.semaphore_wait(barrier, layers + strips - 2)

    twin = group * (1 - half) + place
    near = place // 8 == half
    mine2 = (sec == 2) & (place // 2 == strip)

    def share(lay):
        @pl.when(sec == lay)
        def _():
            if lay != 2:
                for k in range(1, layers):
                    a = (lay + k) % layers
                    remote(
                        staget.at[:, a], hops.at[lay // 2], ssend, srecv.at[lay], strip * layers + a
                    ).start()
                hops[lay // 2] = staget[:, lay]
                return
            for k in range(2):
                peer = group * half + lax.rem(2 * strip, group) + k
                src = stage.at[pl.ds(64 * k, 64)]

                @pl.when(peer != me)
                def _(peer=peer, src=src):
                    remote(src, screen2, ssend, srecv.at[2], peer).start()

                @pl.when(peer == me)
                def _(src=src):
                    screen2[...] = src[...]

    def pass_on(lay):
        if lay == 2:
            @pl.when(near & jnp.logical_not(mine2))
            def _():
                remote(screen2, screen2, ssend, srecv.at[2], me).wait_recv()

            @pl.when(near)
            def _():
                remote(screen2, screen2, fsend.at[2], frecv.at[2], twin).start()
            return
        ref = screen1 if lay == 1 else screen3

        hop = hops.at[lay // 2]

        @pl.when(sec != lay)
        def _():
            remote(hop, hop, ssend, srecv.at[lay], me).wait_recv()

        def one(k, _):
            other = lax.rem(strip + k, strips)
            remote(
                hop.at[lax.rem(other, 4)], ref.at[strip], fsend.at[lay], frecv.at[lay],
                other * layers + sec,
            ).start()
            return 0

        lax.fori_loop(1, strips, one, 0)
        ref[strip] = hop[lax.rem(strip, 4)]

    def passed(lay):
        if lay == 2:
            @pl.when(jnp.logical_not(near))
            def _():
                remote(screen2, screen2, fsend.at[2], frecv.at[2], me).wait_recv()
            return
        some = (screen1 if lay == 1 else screen3).at[pl.ds(0, strips - 1)]
        remote(some, some, fsend.at[lay], frecv.at[lay], me).wait_recv()

    for k in range(1, layers):
        peer = strip * layers + lax.rem(sec + k, layers)
        remote(infos.at[sec], infos.at[sec], isend, irecv, peer).start()

    @pl.when(sec == 0)
    def _():
        for k in range(1, layers):
            remote(
                stage.at[pl.ds(32 * k, 32)], screen0, ssend, srecv.at[0], strip * layers + k
            ).start()
        screen0[...] = stage[0:32, :]

    share(1)

    for k in range(1, layers):
        pl.semaphore_signal(
            ready, inc=1, device_id=(lax.rem(sec + k, layers), strip), device_id_type=MESH
        )

    most = infos.at[pl.ds(0, layers - 1)]
    remote(most, most, isend, irecv, me).wait_recv()
    copies[2].wait()

    dist = infos[3, 8:16, :]
    for lay in range(3):
        dist = jnp.where(row8 // 2 == lay, infos[lay, 8:16, :], dist)
    wide = jnp.concatenate([dist] * 4, axis=1)
    turn = 0.5 / float(1024 * 1024)

    def wave(d, squares):
        t = d * (squares * turn)
        t = t - jnp.round(t)
        sine, cosine_ = sincos(t * (-2.0 * math.pi))
        row = lax.broadcasted_iota(jnp.int32, d.shape, 0)
        return jnp.where(row % 2 == 0, cosine_, sine)

    k = lax.broadcasted_iota(jnp.int32, (8, 512), 1).astype(F32)
    weight = jnp.where(k == 0.0, 0.25, 0.5) / 1024.0
    folded = wave(wide, k * k) * weight
    high = folded.astype(BF16)
    low = (folded - high.astype(F32)).astype(BF16)
    parts = jnp.dot(
        jnp.concatenate([high.astype(F32), low.astype(F32)], axis=0).astype(BF16),
        cosine[...], preferred_element_type=F32,
    )
    last = wave(dist, jnp.full((8, TILE), 512.0 * 512.0, F32)) * (0.25 / 1024.0)
    lane8 = lax.broadcasted_iota(jnp.int32, (8, TILE), 1)
    last = jnp.where(lane8 % 2 == 0, last, -last)
    lines_ref[...] = parts[:8] + parts[8:] + jnp.concatenate([last] * 8, axis=1)

    def build(lay):
        quarters = []
        for q in range(4):
            at = slice(QUARTER * q, QUARTER * (q + 1))
            quarters.append((
                lines_ref[2 * lay:2 * lay + 1, at], lines_ref[2 * lay + 1:2 * lay + 2, at]
            ))
        for b, (re, im) in enumerate(spread(quarters)):
            turned = [(re, im), (-im, re), (-re, -im), (im, -re)][b]
            for part, (first, second) in enumerate([(turned[0], re), (turned[1], im)]):
                row = jnp.concatenate([first, second], axis=1)
                base = pltpu.roll(
                    jnp.broadcast_to(row, (TILE, 2 * QUARTER)), 0, axis=1, stride=1, stride_axis=0
                ).astype(BF16)
                gmat[lay, b, part, 0:TILE, :] = base[:, 2 * TILE:4 * TILE]
                gmat[lay, b, part, TILE:2 * TILE, :] = base[:, TILE:3 * TILE]

    def angles(lay):
        if lay == 0:
            @pl.when(sec != 0)
            def _():
                remote(screen0, screen0, ssend, srecv.at[0], me).wait_recv()

            for r in range(0, 32, PIECE):
                sine, cosine_ = sincos(screen0[r:r + PIECE, :].astype(F32))
                sincos_ref[0, r:r + PIECE, :] = sine
                sincos_ref[1, r:r + PIECE, :] = cosine_
            return
        passed(lay)
        if lay == 2:
            for r in range(0, 64, PIECE):
                sine, cosine_ = sincos(screen2[r:r + PIECE, :].astype(F32))
                sincos_ref[0, r:r + PIECE, :] = sine
                sincos_ref[1, r:r + PIECE, :] = cosine_
            return
        ref = screen1 if lay == 1 else screen3
        for s in range(strips):
            sine, cosine_ = sincos(ref[s].astype(F32))
            sincos_ref[0, :, TILE * s:TILE * (s + 1)] = sine
            sincos_ref[1, :, TILE * s:TILE * (s + 1)] = cosine_

    def put(b, re_at, im_at, c, re, im):
        lanes = slice(TILE * c, TILE * (c + 1))
        re = re.astype(BF16)
        im = im.astype(BF16)
        slab[b, re_at:re_at + PIECE, lanes] = re
        slab[b, im_at:im_at + PIECE, lanes] = im
        swapped[b, re_at:re_at + PIECE, lanes] = -im
        swapped[b, im_at:im_at + PIECE, lanes] = re

    def put_all(re_at, im_at, c, x):
        for b, (re, im) in enumerate(spread(x)):
            put(b, re_at, im_at, c, re, im)

    def pieces(split):
        if split:
            return [(r, 64 + r, r) for r in range(0, 64, PIECE)]
        return [(64 * f + r, 64 * f + 32 + r, r) for f in range(2) for r in range(0, 32, PIECE)]

    def screened(x, line, c):
        out = []
        for q, (re, im) in enumerate(x):
            lanes = slice(QUARTER * q + TILE * c, QUARTER * q + TILE * (c + 1))
            sine = sincos_ref[0, line:line + PIECE, lanes]
            cosine_ = sincos_ref[1, line:line + PIECE, lanes]
            out.append((re * cosine_ - im * sine, re * sine + im * cosine_))
        return out

    def finished(re_at, im_at, c):
        lanes = slice(TILE * c, TILE * (c + 1))
        return collect([
            (ybuf[b, re_at:re_at + PIECE, lanes], ybuf[b, im_at:im_at + PIECE, lanes])
            for b in range(4)
        ])

    def along(lay, first=0, number=TILE):
        at = slice(first, first + number)
        for b in range(4):
            ybuf[b, at, :] = jnp.dot(
                slab[b, at, :], gmat[lay, b, 0], preferred_element_type=F32
            ) + jnp.dot(swapped[b, at, :], gmat[lay, b, 1], preferred_element_type=F32)

    lane = lax.broadcasted_iota(jnp.int32, (32, TILE), 1)
    lower = lane < 64

    def across(lay, store, targets, send, recv, slot, step):
        dims = (((1,), (1,)), ((), ()))
        for chunk in range(2):
            at = slice(TILE * chunk, TILE * (chunk + 1))
            y = [
                lax.dot_general(
                    gmat[lay, (4 - b) % 4, 0, at, :], slab[b], dims, preferred_element_type=F32
                ) + lax.dot_general(
                    gmat[lay, (4 - b) % 4, 1, at, :], swapped[b], dims, preferred_element_type=F32
                )
                for b in range(4)
            ]
            for r in range(0, TILE, 32):
                y0, y1, y2, y3 = [v[r:r + 32, :] for v in y]
                even, odd, both, gap = y0 + y2, y0 - y2, y1 + y3, y1 - y3
                if step == 0:
                    turned = jnp.where(
                        lane % 64 < 32, -pltpu.roll(gap, TILE - 32, axis=1), pltpu.roll(gap, 32, axis=1)
                    )
                else:
                    moved = pltpu.roll(gap, 64, axis=1)
                    turned = jnp.where(lower, -moved, moved)
                for q, v in enumerate([even + both, odd - turned, even - both, odd + turned]):
                    store(q, chunk, r, v)

            def one(i, _, chunk=chunk):
                dev, index = targets(lax.rem(i + me, 16 if step in (0, 3) else 8), chunk)

                @pl.when(dev != me)
                def _():
                    src, dst = (send.at[0], recv.at[0]) if step == 3 else (send, recv)
                    remote(
                        src.at[index], dst.at[slot], xsend.at[step], xrecv.at[step], dev
                    ).start()
                return 0

            lax.fori_loop(0, 16 if step in (0, 3) else 8, one, 0)

        if step == 3:
            def late(i, _):
                dev = lax.rem(i + me, count)
                remote(
                    send.at[1, dev], recv.at[1, me], xsend.at[4], xrecv.at[4], dev
                ).start()
                return 0

            lax.fori_loop(1, count, late, 0)

    held = {}

    def store_first(q, chunk, r, v):
        p = 4 * q + 2 * chunk + r // 64
        if r % 64 == 0:
            held[q] = v
            return
        top, bottom = held[q], v
        send1[p] = jnp.where(lower, top, pltpu.roll(bottom, 64, axis=1)).astype(BF16)
        send1[group + p] = jnp.where(lower, pltpu.roll(top, 64, axis=1), bottom).astype(BF16)

    def targets_first(i, chunk):
        dev = group * (i // 8) + 4 * lax.rem(i // 2, 4) + 2 * chunk + lax.rem(i, 2)
        return dev, dev

    def store_middle(send):
        def store(q, chunk, r, v):
            send[4 * q + 2 * chunk + r // 64, r % 64:r % 64 + 32, :] = v.astype(BF16)
        return store

    def targets_middle(i, chunk):
        p = 4 * (i // 2) + 2 * chunk + lax.rem(i, 2)
        return group * half + p, p

    def store_last(q, chunk, r, v):
        for n in range(2):
            send4[n, 8 * q + 4 * chunk + r // 32] = v[16 * n:16 * (n + 1), :].astype(BF16)

    def targets_last(i, chunk):
        dev = 8 * (i // 4) + 4 * chunk + lax.rem(i, 4)
        return dev, dev

    def wait_arrival(recv, number, step):
        some = recv.at[pl.ds(0, number)]
        remote(some, some, xsend.at[step], xrecv.at[step], me).wait_recv()

    def arrive_first():
        recv1[me] = send1[me]
        wait_arrival(recv1, count - 1, 0)
        small = lax.broadcasted_iota(jnp.int32, (PIECE, TILE), 1) // 32
        for c in range(2):
            for r in range(0, 32, PIECE):
                tiles = []
                for q in range(4):
                    g = 2 * q + c
                    got = [recv1[4 * g + s, r:r + PIECE, :].astype(F32) for s in range(4)]
                    outs = []
                    for fc in range(4):
                        out = None
                        for s in range(4):
                            shift = ((s - fc) * 32) % TILE
                            moved = pltpu.roll(got[s], shift, axis=1) if shift else got[s]
                            out = moved if out is None else jnp.where(small == s, moved, out)
                        outs.append(out)
                    tiles.append(outs)
                for e in range(2):
                    at = 32 * e + r
                    put_all(at, 64 + at, c, [(t[2 * e], t[2 * e + 1]) for t in tiles])

    low16 = lax.broadcasted_iota(jnp.int32, (PIECE, TILE), 1) < 64

    def joined(recv, base, g, r):
        one = recv[base + 2 * g, r:r + PIECE, :].astype(F32)
        two = recv[base + 2 * g + 1, r:r + PIECE, :].astype(F32)
        return (
            jnp.where(low16, one, pltpu.roll(two, 64, axis=1)),
            jnp.where(low16, pltpu.roll(one, 64, axis=1), two),
        )

    def arrive_middle(send, recv, step):
        recv[place] = send[place]
        wait_arrival(recv, group - 1, step)
        for c in range(2):
            for r in range(0, 64, PIECE):
                put_all(r, 64 + r, c, [joined(recv, 0, 2 * q + c, r) for q in range(4)])

    def arrive_last(n):
        recv, send = recv4.at[n], send4.at[n]
        recv[me] = send[me]
        wait_arrival(recv, count - 1, 3 + n)
        for c in range(2):
            for f in range(2):
                at = 64 * n + 32 * f
                put_all(
                    at, at + 16, c, [joined(recv, group * f, 2 * q + c, 0) for q in range(4)]
                )

    def rescreen():
        for c in range(2):
            for re_at, im_at, line in pieces(True):
                put_all(re_at, im_at, c, screened(finished(re_at, im_at, c), line, c))

    build(0)
    copies[1].wait()
    pass_on(1)
    angles(0)
    for c in range(2):
        for n, (re_at, im_at, line) in enumerate(pieces(False)):
            f = n // 2
            x = []
            for q in range(4):
                lanes = slice(QUARTER * q + TILE * c, QUARTER * q + TILE * (c + 1))
                x.append((
                    field[2 * f, line:line + PIECE, lanes].astype(F32),
                    field[2 * f + 1, line:line + PIECE, lanes].astype(F32),
                ))
            put_all(re_at, im_at, c, screened(x, line, c))
    pl.semaphore_wait(ready, layers - 1)
    across(0, store_first, targets_first, send1, recv1, me, 0)

    share(2)
    share(3)
    for lay in range(1, layers):
        build(lay)
    pick = jnp.concatenate([infos[a, 0:8, :] for a in range(layers)], axis=0)
    block_row = jnp.floor(pick * (1.0 / 64.0))
    left = (pick - 64.0 * block_row) * 16.0
    low_row = block_row - (2 * sec).astype(F32)
    left = jnp.where((low_row == 0.0) | (low_row == 1.0), left, -4096.0)
    lane_f = lane.astype(F32)
    for k in range(SUB):
        for t in range(8):
            select[32 * k:32 * (k + 1), TILE * t:TILE * (t + 1)] = jnp.where(
                lane_f + float(TILE * t - k) == left, 1.0, 0.0
            ).astype(BF16)

    angles(1)
    arrive_first()
    along(0)
    rescreen()
    across(1, store_middle(send2), targets_middle, send2, recv2, place, 1)
    pass_on(2)
    pass_on(3)
    angles(2)
    arrive_middle(send2, recv2, 1)
    along(1)
    rescreen()
    across(2, store_middle(send3), targets_middle, send3, recv3, place, 2)
    angles(3)
    arrive_middle(send3, recv3, 2)
    along(2)
    rescreen()
    across(3, store_last, targets_last, send4, recv4, me, 3)
    beside = strip * layers + sec + 1 - 2 * lax.rem(sec, 2)
    above = strip * layers + lax.rem(sec + 2, layers)

    def rows_of(n, owner):
        return pl.ds(pl.multiple_of(32 * owner + 16 * n, 16), 16)

    def keep(first, number, rows):
        part = (pl.ds(first, number), rows)
        pltpu.make_async_copy(pupil.at[part], out_ref.at[part], wsem).start()

    def publish(n):
        own = rows_of(n, sec)
        for fc in range(4):
            f, part = fc // 2, fc % 2
            pupil[fc, own, :] = mine[64 * f + 32 * part + 16 * n:64 * f + 32 * part + 16 * n + 16, :]
        for k in range(2):
            part = pupil.at[pl.ds(2 * k, 2), own]
            remote(part, part, osend.at[n, 0, k], orecv.at[n, 0, k], beside).start()
            part = pupil.at[pl.ds(2 - 2 * k, 2), own]
            remote(part, part, osend.at[n, 1, k], orecv.at[n, 1, k], above).start()
        keep(0, 4, own)

    def relay(n):
        part = pupil.at[pl.ds(0, 2), rows_of(n, sec)]
        remote(part, part, osend.at[n, 0, 0], orecv.at[n, 0, 0], me).wait_recv()
        rows = rows_of(n, sec + 1 - 2 * lax.rem(sec, 2))
        given = pupil.at[pl.ds(0, 2), rows]
        remote(given, given, osend.at[n, 2, 0], orecv.at[n, 2, 0], above).start()
        keep(0, 2, rows)
        remote(part, part, osend.at[n, 1, 0], orecv.at[n, 1, 0], me).wait_recv()
        rows = rows_of(n, lax.rem(sec + 2, layers))
        given = pupil.at[pl.ds(2, 2), rows]
        remote(given, given, osend.at[n, 2, 1], orecv.at[n, 2, 1], beside).start()
        keep(2, 2, rows)

    for n in range(2):
        arrive_last(n)
        along(3, 64 * n, 64)
        for c in range(2):
            for f in range(2):
                at = 64 * n + 32 * f
                for q, (re, im) in enumerate(finished(at, at + 16, c)):
                    lanes = slice(QUARTER * q + TILE * c, QUARTER * q + TILE * (c + 1))
                    to = 64 * f + 16 * n
                    mine[to:to + PIECE, lanes] = re.astype(BF16)
                    mine[to + 32:to + 32 + PIECE, lanes] = im.astype(BF16)
        publish(n)
    relay(0)

    copies[3].wait()
    copies[4].wait()
    lane_row = lax.rem(lane // SUB, 2)
    match = lane_row.astype(F32) == low_row
    dims = (((1,), (1,)), ((), ()))
    taken = lax.dot_general(select[...], mine[...], dims, preferred_element_type=F32)
    folds = []
    for k in range(0, SUB, 2):
        x = jnp.where(match, taken[32 * k:32 * (k + 1), :], 0.0)
        x2 = jnp.where(match, taken[32 * (k + 1):32 * (k + 2), :], 0.0)
        x = x + pltpu.roll(x, TILE - SUB, axis=1)
        x2 = x2 + pltpu.roll(x2, SUB, axis=1)
        folds.append(jnp.where(lane_row == 0, x, x2))
    for m in range(4):
        c0, c1 = folds[2 * m], folds[2 * m + 1]
        lanes = slice(TILE * m, TILE * (m + 1))
        flat[0:32, lanes] = jnp.where(lower, c0, pltpu.roll(c1, 64, axis=1)).astype(BF16)
        flat[32:64, lanes] = jnp.where(lower, pltpu.roll(c0, 64, axis=1), c1).astype(BF16)
    total = jnp.zeros((64, 16), F32)
    for n in range(4):
        at = slice(256 * n, 256 * (n + 1))
        past = slice(1024 + 256 * n, 1024 + 256 * (n + 1))
        re = jnp.dot(flat[...], spot[:, at], preferred_element_type=F32)
        im = jnp.dot(flat[...], spot[:, past], preferred_element_type=F32)
        total = total + lax.dot_general(
            (re * re + im * im).astype(BF16), templates_ref[:, at], dims, preferred_element_type=F32
        )
    for f in range(2):
        results[:, f, 0:16] = total[32 * f:32 * (f + 1), :]

    def answer(i, _):
        dev = lax.rem(me + i, count)
        index = 8 * lax.rem(dev, layers) + dev // layers
        remote(results.at[index], answers.at[me], csend, crecv, dev).start()
        return 0

    lax.fori_loop(1, count, answer, 0)
    answers[me] = results[8 * sec + strip]

    relay(1)
    for n in range(2):
        part = pupil.at[pl.ds(0, 2), rows_of(n, sec)]
        owners = (sec + 1 - 2 * lax.rem(sec, 2), lax.rem(sec + 2, layers), layers - 1 - sec)
        for way, k, first in ((0, 1, 2), (1, 1, 0), (2, 0, 0), (2, 1, 2)):
            remote(part, part, osend.at[n, way, k], orecv.at[n, way, k], me).wait_recv()
            keep(first, 2, rows_of(n, owners[way]))
    some = answers.at[pl.ds(0, count - 1)]
    remote(some, some, csend, crecv, me).wait()
    for s in range(strips):
        block = answers[layers * s]
        for a in range(1, layers):
            block = block + answers[layers * s + a]
        corr_ref[s] = block[0:2, 0:16]

    part = pupil.at[pl.ds(0, 2), rows_of(0, sec)]
    for n in range(2):
        for k in range(2):
            for way in range(3):
                remote(part, part, osend.at[n, way, k], orecv.at[n, way, k], me).wait_send()
    pltpu.make_async_copy(pupil, out_ref, wsem).wait()

    some = infos.at[pl.ds(0, layers - 1)]
    remote(some, some, isend, irecv, me).wait_send()

    @pl.when(sec == 0)
    def _():
        some = stage.at[pl.ds(0, 96)]
        remote(some, some, ssend, srecv.at[0], me).wait_send()

    @pl.when(lax.rem(sec, 2) == 1)
    def _():
        some = columns.at[pl.ds(0, 12)]
        remote(some, some, ssend, srecv.at[1], me).wait_send()

    @pl.when((sec == 2) & mine2)
    def _():
        remote(screen2, screen2, ssend, srecv.at[2], me).wait_send()

    @pl.when((sec == 2) & jnp.logical_not(mine2))
    def _():
        remote(stage, stage, ssend, srecv.at[2], me).wait_send()

    @pl.when(near)
    def _():
        remote(screen2, screen2, fsend.at[2], frecv.at[2], me).wait_send()

    for lay, ref in ((1, screen1), (3, screen3)):
        some = ref.at[pl.ds(0, strips - 1)]
        remote(some, some, fsend.at[lay], frecv.at[lay], me).wait_send()

    for step, (send, number) in enumerate(
        [(send1, count), (send2, group), (send3, group), (send4.at[0], count), (send4.at[1], count)]
    ):
        some = send.at[pl.ds(0, number - 1)]
        remote(some, some, xsend.at[step], xrecv.at[step], me).wait_send()


def fused(launch, screens, distance, templates, send_table, send_counts):
    rows, length = launch.shape[2:]
    vmem = pl.BlockSpec(memory_space=pltpu.VMEM)
    smem = pl.BlockSpec(memory_space=pltpu.SMEM)
    far = pl.BlockSpec(memory_space=pltpu.HBM)
    dma = pltpu.SemaphoreType.DMA

    def blocks(number, height):
        return pltpu.VMEM((number, height, TILE), BF16)

    return pl.pallas_call(
        fused_kernel,
        out_shape=(
            jax.ShapeDtypeStruct((4, rows, length), BF16),
            jax.ShapeDtypeStruct((8, 2, 16), F32),
        ),
        in_specs=[smem, smem, smem, far, far, far, far, far],
        out_specs=(far, vmem),
        scratch_shapes=[
            pltpu.VMEM(templates.shape[::-1], BF16),
            pltpu.VMEM((4, 32, length), BF16),
            pltpu.VMEM((rows, length), F32),
            pltpu.VMEM((length // 2, length), BF16),
            pltpu.VMEM((512, 2048), BF16),
            pltpu.VMEM((4, 16, TILE), F32),
            pltpu.VMEM((8, length), F32),
            pltpu.VMEM((4, 4, 2, QUARTER, QUARTER), BF16),
            pltpu.VMEM((rows, length), BF16),
            pltpu.VMEM((4, 4, 64, TILE), BF16),
            pltpu.VMEM((2, 4, 64, TILE), BF16),
            pltpu.VMEM((32, length), BF16),
            pltpu.VMEM((16, 64, TILE), BF16),
            pltpu.VMEM((64, length), BF16),
            pltpu.VMEM((2, 64, length), F32),
            pltpu.VMEM((4, TILE, QUARTER), BF16),
            pltpu.VMEM((4, TILE, QUARTER), BF16),
            pltpu.VMEM((4, TILE, QUARTER), F32),
            blocks(32, 32), blocks(32, 32),
            blocks(16, 64), blocks(16, 64),
            blocks(16, 64), blocks(16, 64),
            pltpu.VMEM((2, 32, 16, TILE), BF16), pltpu.VMEM((2, 32, 16, TILE), BF16),
            pltpu.VMEM((TILE, length), BF16),
            pltpu.VMEM((4, rows, length), BF16),
            pltpu.VMEM((512, length), BF16),
            pltpu.VMEM((64, 512), BF16),
            pltpu.VMEM((32, 2, TILE), F32),
            pltpu.VMEM((32, 2, TILE), F32),
            dma((5,)), pltpu.SemaphoreType.REGULAR, dma, dma, dma, dma((4,)), dma((4,)), dma((4,)),
            dma((5,)), dma((5,)), dma((2, 3, 2)), dma((2, 3, 2)), dma, dma, dma,
        ],
        compiler_params=pltpu.CompilerParams(
            collective_id=2, has_side_effects=True, vmem_limit_bytes=60 << 20
        ),
        name="fused",
    )(
        send_table.reshape(8), send_counts.reshape(8), distance, templates.T, launch.reshape(4, 4, 32, length), screens[0],
        jnp.asarray(cosine_half_table(length)), jnp.asarray(spot_rows(SUB)),
    )


def finish_kernel(pupil_ref, found_ref, pupil_out, found_out, pupil, found, gets, puts):
    pairs = [(found_ref, found, found_out)]
    pairs += [(pupil_ref.at[n], pupil.at[n], pupil_out.at[n]) for n in range(4)]
    reads = [pltpu.make_async_copy(s, m, gets.at[n]) for n, (s, m, _) in enumerate(pairs)]
    writes = [pltpu.make_async_copy(m, d, puts.at[n]) for n, (_, m, d) in enumerate(pairs)]
    for copy in reads:
        copy.start()
    for read, write in zip(reads, writes):
        read.wait()
        write.start()
    for write in writes:
        write.wait()


def finish(pupil, found):
    far = pl.BlockSpec(memory_space=pltpu.HBM)
    dma = pltpu.SemaphoreType.DMA
    return pl.pallas_call(
        finish_kernel,
        out_shape=tuple(jax.ShapeDtypeStruct(x.shape, x.dtype) for x in (pupil, found)),
        in_specs=[far, far],
        out_specs=(far, far),
        scratch_shapes=[
            pltpu.VMEM(pupil.shape, pupil.dtype), pltpu.VMEM(found.shape, found.dtype),
            dma((5,)), dma((5,)),
        ],
        compiler_params=pltpu.CompilerParams(vmem_limit_bytes=60 << 20),
        name="finish",
    )(pupil, found)


def per_device_fused(launch, screens, distance, templates, send_table, send_counts):
    rows, length = launch.shape[2:]
    pupil, found = finish(
        *fused(launch, screens, distance, templates, send_table, send_counts)
    )
    return pupil.reshape(2, 2, rows, length), found[None, :, None]


def per_device(launch, screens, distance, templates, send_table, send_counts):
    layers = lax.axis_size("layer")
    strips = lax.axis_size("strip")
    sec = lax.axis_index("layer")
    fields = launch.shape[0]
    rows, length = launch.shape[2:]
    line = kernel_line(distance[0], length)
    done = propagate(launch, screens, line, layers, strips)
    pupil = done.transpose(1, 0, 2, 3).reshape(fields, 2, rows, length)
    side = length // SUB
    blocks = gather_blocks(pupil.reshape(2 * fields, rows, length), send_table.reshape(strips))
    flat = blocks.reshape(strips * fields, 2 * SUB * SUB)
    table = jnp.asarray(spot_table(SUB))
    pixels = templates.shape[0]
    spot = jnp.dot(flat, table, preferred_element_type=F32)
    intensity = (spot[:, :pixels] ** 2 + spot[:, pixels:] ** 2).astype(BF16)
    result = jnp.dot(intensity, templates, preferred_element_type=F32)
    result = result.reshape(strips, fields, templates.shape[1])
    live = sec < send_counts[0]
    result = jnp.where(live[:, None, None], result, 0.0)
    received = swap_strips(result, strips)
    return (pupil, received[None, :, None])


def solution(mesh):
    placed = (
        P(None, None, "strip", None),
        P("layer", "strip", None),
        P("layer"),
        P(),
        P("strip", None, "layer"),
        P("strip", None),
    )
    small = mesh.shape["layer"] == 4 and mesh.shape["strip"] == 8
    return jax.shard_map(
        per_device_fused if small else per_device,
        mesh=mesh,
        in_specs=placed,
        out_specs=(P(None, None, "strip", None), P("strip", None, "layer", None, None)),
        check_vma=False,
    )
```
